32 devices in a mesh: groups: 2 (over x), ctx: 16 (over z, y, core).
Axes of the slice: x: 2, y: 2, z: 4, core: 2. Of those that a mesh axis runs over, the one named last changes fastest.
Arguments:
- queries: bfloat16 [256, 8192], P(('groups', 'ctx')), parts along dimension 0, may hold values from -8 to 8
- prefix_key_heads: bfloat16 [16384, 1024], P(('groups', 'ctx')), parts along dimension 0, may hold values from -8 to 8
- prefix_value_heads: bfloat16 [16384, 1024], P(('groups', 'ctx')), parts along dimension 0, may hold values from -6 to 6
- tree_key_heads: bfloat16 [256, 1024], P(('groups', 'ctx')), parts along dimension 0, may hold values from -16 to 16
- tree_value_heads: bfloat16 [256, 1024], P(('groups', 'ctx')), parts along dimension 0, may hold values from -6 to 6
- token_embed: bfloat16 [256, 8192], P(('groups', 'ctx')), parts along dimension 0, may hold values from -12 to 12
- fc_embed: bfloat16 [8192, 8192], P('ctx'), may hold values from -0.25 to 0.25
- fc_feature: bfloat16 [8192, 8192], P('ctx'), may hold values from -0.0625 to 0.0625
- draft_gain: float32 [8192], replicated, may hold values from 0.5 to 1.5
- parents: int32 [4, 64], P('groups'), parts along dimension 0, may hold values from 0 to 62, as said below
- accepted: int32 [4], P('groups'), parts along dimension 0, may hold values from 0 to 63, as said below
Outputs:
- attended: bfloat16 [256, 8192], P(('groups', 'ctx')), parts along dimension 0
- draft_input: bfloat16 [256, 8192], P(('groups', 'ctx')), parts along dimension 0
The draws below stay inside these ranges and needn't reach their ends.
There are 2 independent parts, one for each index of `groups`. The reference program is written for one: setup_inputs(seed, part) draws one part's arguments, and reference() takes and returns one part's arrays. A program takes and returns all parts, laid end to end along the dimension named above; an argument that names none is the same for every part. Nothing has to cross between parts.
Inputs may be any that keep to these rules, and one draw needn't show every extreme that they name: parents[t, 0] = 0 marks the root; every other node's parent is an earlier node of the same tree; no node lies more than 6 steps below its root, and every tree has a node exactly 6 steps below it. The accepted rows of tree t are node accepted[t] and all its ancestors, so at most 7 rows a tree; in every draw some tree accepts exactly 7 rows.
All inputs are finite; a program needn't handle non-finite values.
Results may differ from the reference program's by a relative error of at most 0.0028.
Values may be sent and summed in bfloat16 or wider, within the bound.
No kernel may reach another device: no remote copies, remote signals or barrier semaphores. Data moves between devices by JAX's collectives and lax.ppermute only.
A program may use at most 128 MiB of HBM per device.

```python
import jax
import jax.numpy as jnp
from jax import lax

D = 8192
QUERY_HEADS = 64
KEY_HEADS = 8
HEAD_WIDTH = 128
TREE_NODES = 64
ACC = 7
DRAFT_TREES = 2
PREFIX_PER_SHARD = 512
TREE_ROW_TOTAL = 128
PREFIX_LENGTH = 8192
N_CTX = 16


def query_block(key):
    base_key = jax.random.fold_in(key, 11)
    key_scale, key_value_pair = jax.random.split(base_key)
    row_scaling = jnp.exp(jax.random.uniform(key_scale, (TREE_ROW_TOTAL, 1, 1), minval=jnp.log(0.4), maxval=jnp.log(4.0)))
    value_rows = jax.random.normal(key_value_pair, (TREE_ROW_TOTAL, QUERY_HEADS, HEAD_WIDTH))
    queries = jnp.clip(value_rows * row_scaling, -8.0, 8.0)
    return (queries, row_scaling)


def draw_queries(key, part):
    queries, row_scaling = query_block(key)
    return queries.reshape(TREE_ROW_TOTAL, QUERY_HEADS * HEAD_WIDTH).astype(jnp.bfloat16)


def draw_tree_key_heads(key, part):
    queries, row_scaling = query_block(key)
    queries_per_group = QUERY_HEADS // KEY_HEADS
    grouped_heads = jnp.sum(queries.reshape(TREE_ROW_TOTAL, KEY_HEADS, queries_per_group, HEAD_WIDTH), axis=2) / row_scaling
    jitter_portion = jax.random.normal(jax.random.fold_in(key, 12), (TREE_ROW_TOTAL, KEY_HEADS, HEAD_WIDTH))
    tree_key_rows = 2.5 * grouped_heads / jnp.sqrt(1.0 * queries_per_group) + 0.5 * jitter_portion
    return jnp.clip(tree_key_rows, -16.0, 16.0).reshape(TREE_ROW_TOTAL, KEY_HEADS * HEAD_WIDTH).astype(jnp.bfloat16)


def draw_prefix_key_heads(key, part):
    base_key = jax.random.fold_in(key, 21)
    key_scale, key_value_pair = jax.random.split(base_key)
    position_scale = jnp.exp(jax.random.uniform(key_scale, (PREFIX_LENGTH, 1, 1), minval=jnp.log(0.25), maxval=jnp.log(2.5)))
    value_rows = jax.random.normal(key_value_pair, (PREFIX_LENGTH, KEY_HEADS, HEAD_WIDTH))
    prefix_key_rows = jnp.clip(value_rows * position_scale, -8.0, 8.0)
    return prefix_key_rows.reshape(PREFIX_LENGTH, KEY_HEADS * HEAD_WIDTH).astype(jnp.bfloat16)


def draw_prefix_value_heads(key, part):
    base_key = jax.random.fold_in(key, 31)
    key_averages, key_jitter = jax.random.split(base_key)
    region_averages = jax.random.normal(key_averages, (8, KEY_HEADS * HEAD_WIDTH))
    region_of = jnp.arange(PREFIX_LENGTH, dtype=jnp.int32) * 8 // PREFIX_LENGTH
    jitter_portion = 0.7 * jax.random.normal(key_jitter, (PREFIX_LENGTH, KEY_HEADS * HEAD_WIDTH))
    return jnp.clip(region_averages[region_of] + jitter_portion, -6.0, 6.0).astype(jnp.bfloat16)


def draw_token_embed(key, part):
    base_key = jax.random.fold_in(key, 41)
    key_scale, key_value_pair = jax.random.split(base_key, 2)
    row_scaling = jnp.exp(jax.random.uniform(key_scale, (TREE_ROW_TOTAL, 1), minval=jnp.log(0.3), maxval=jnp.log(3.0)))
    value_rows = jax.random.normal(key_value_pair, (TREE_ROW_TOTAL, D))
    return jnp.clip(value_rows * row_scaling, -12.0, 12.0).astype(jnp.bfloat16)


def draw_fc_embed(key, part):
    base_key = jax.random.fold_in(key, 51)
    key_scale, key_value_pair = jax.random.split(base_key)
    column_scale = jnp.exp(jax.random.uniform(key_scale, (1, D), minval=jnp.log(0.3), maxval=jnp.log(3.0)))
    value_rows = jax.random.normal(key_value_pair, (D, D))
    return jnp.clip(value_rows * column_scale / jnp.sqrt(1.0 * D), -0.25, 0.25).astype(jnp.bfloat16)


def tree_shapes(key):
    base_key = jax.random.fold_in(key, 61)
    tree_keys_all = jax.random.split(base_key, DRAFT_TREES)

    def one_tree(tree_key):
        key_chain, key_pick = jax.random.split(tree_key)
        shuffled = jax.random.permutation(key_chain, TREE_NODES - 1).astype(jnp.int32) + 1
        chain_nodes = jnp.sort(shuffled[:ACC - 1])
        chain_prev = jnp.concatenate([jnp.zeros((1,), jnp.int32), chain_nodes[:-1]])
        on_chain = (jnp.arange(TREE_NODES, dtype=jnp.int32)[:, None] == chain_nodes[None, :]).astype(jnp.int32)
        chain_parent = jnp.sum(on_chain * chain_prev[None, :], axis=1)
        is_chain = jnp.sum(on_chain, axis=1) > 0
        ranking = jax.random.randint(key_pick, (TREE_NODES, TREE_NODES), 0, 1 << 20) * TREE_NODES + jnp.arange(TREE_NODES, dtype=jnp.int32)[None, :]

        def attach(depth_now, node_index):
            eligible = (jnp.arange(TREE_NODES, dtype=jnp.int32) < node_index) & (depth_now < ACC - 1)
            picked = jnp.argmax(jnp.where(eligible, ranking[node_index], -1)).astype(jnp.int32)
            parent = jnp.where(is_chain[node_index], chain_parent[node_index], picked)
            depth_now = depth_now.at[node_index].set(depth_now[parent] + 1)
            return (depth_now, parent)
        depth_start = jnp.zeros((TREE_NODES,), jnp.int32)
        depth_end, later_parents = lax.scan(attach, depth_start, jnp.arange(1, TREE_NODES, dtype=jnp.int32))
        tree_parents = jnp.concatenate([jnp.zeros((1,), jnp.int32), later_parents])
        return (tree_parents, chain_nodes[ACC - 2])
    return jax.vmap(one_tree)(tree_keys_all)


def draw_parents(key, part):
    tree_parents, chain_end = tree_shapes(key)
    return tree_parents.astype(jnp.int32)


def draw_accepted(key, part):
    tree_parents, chain_end = tree_shapes(key)
    base_key = jax.random.fold_in(key, 71)
    key_nodes, key_full = jax.random.split(base_key)
    random_nodes = jax.random.randint(key_nodes, (DRAFT_TREES,), 0, TREE_NODES)
    full_tree = jax.random.randint(key_full, (), 0, DRAFT_TREES)
    return jnp.where(jnp.arange(DRAFT_TREES, dtype=jnp.int32) == full_tree, chain_end, random_nodes).astype(jnp.int32)


def levels(key, extent, cuts, least, largest):
    loudness = 1.0
    for position, shards_of in cuts:
        heights = jax.random.uniform(jax.random.fold_in(jax.random.fold_in(key, 6), position), (shards_of,), jnp.float32, least / len(cuts), largest / len(cuts))
        loudness = loudness * jnp.repeat(jnp.exp(heights), extent[position] // shards_of).reshape((-1,) + (1,) * (len(extent) - 1 - position))
    return loudness


def scatter_about(rng, dims, scale, limit, pieces=(), kind=jnp.bfloat16):
    loudness = levels(rng, dims, pieces, -0.22, 0.18) if pieces else 1.0
    drawn = jax.random.normal(rng, dims, jnp.float32) * scale * loudness
    return jnp.minimum(jnp.maximum(drawn, -limit), limit).astype(kind)


def setup_inputs(seed: int = 0, part: int = 0) -> dict:
    keys = jax.random.split(jax.random.key(seed), 12)
    own_keys = jax.random.split(jax.random.fold_in(keys[11], part), 12)
    return {
        "queries": draw_queries(jax.random.fold_in(jax.random.fold_in(keys[11], part), 71), part),
        "prefix_key_heads": draw_prefix_key_heads(jax.random.fold_in(jax.random.fold_in(keys[11], part), 71), part),
        "prefix_value_heads": draw_prefix_value_heads(jax.random.fold_in(jax.random.fold_in(keys[11], part), 71), part),
        "tree_key_heads": draw_tree_key_heads(jax.random.fold_in(jax.random.fold_in(keys[11], part), 71), part),
        "tree_value_heads": scatter_about(own_keys[4], (TREE_ROW_TOTAL, KEY_HEADS * HEAD_WIDTH), 1.0, 6.0, ((0, 16),)),
        "token_embed": draw_token_embed(jax.random.fold_in(jax.random.fold_in(keys[11], part), 71), part),
        "fc_embed": draw_fc_embed(jax.random.fold_in(keys[11], 71), part),
        "fc_feature": scatter_about(keys[7], (D, D), D ** -0.5, 0.0625, ((0, 16),)),
        "draft_gain": jnp.clip(1.0 + 0.1 * jax.random.normal(keys[8], (D,), jnp.float32), 0.5, 1.5),
        "parents": draw_parents(jax.random.fold_in(jax.random.fold_in(keys[11], part), 71), part),
        "accepted": draw_accepted(jax.random.fold_in(jax.random.fold_in(keys[11], part), 71), part),
    }


highest = lax.Precision.HIGHEST
negative_fill = -1e+30

def ancestors(parents):
    nodes = parents.shape[1]
    column = jnp.arange(nodes, dtype=jnp.int32)
    upward = (parents[:, :, None] == column[None, None, :]).astype(jnp.float32)
    closure = jnp.maximum(upward, jnp.eye(nodes, dtype=jnp.float32)[None])
    for repeat in range(max(1, (nodes - 1).bit_length())):
        closure = jnp.minimum(jnp.einsum('tij,tjk->tik', closure, closure, precision=highest), 1.0)
    return closure

def path_rows(closure, accepted):
    nodes = closure.shape[1]
    chosen = (accepted[:, None] == jnp.arange(nodes, dtype=jnp.int32)[None, :]).astype(jnp.float32)
    return jnp.einsum('ti,tij->tj', chosen, closure, precision=highest)

def reference(queries, prefix_key_heads, prefix_value_heads, tree_key_heads, tree_value_heads, token_embed, fc_embed, fc_feature, draft_gain, parents, accepted):
    every_row = DRAFT_TREES * TREE_NODES
    queries_per_group = QUERY_HEADS // KEY_HEADS
    scale_factor = HEAD_WIDTH ** (-0.5)
    grouped_query = queries.astype(jnp.float32).reshape(every_row, KEY_HEADS, queries_per_group, HEAD_WIDTH)

    def block_step(carry, block_index):
        run_max, run_num, run_den = carry
        leading_rows = (block_index * PREFIX_PER_SHARD).astype(jnp.int32)
        key_block_slice = lax.dynamic_slice_in_dim(prefix_key_heads, leading_rows, PREFIX_PER_SHARD, 0).astype(jnp.float32).reshape(PREFIX_PER_SHARD, KEY_HEADS, HEAD_WIDTH)
        value_block_slice = lax.dynamic_slice_in_dim(prefix_value_heads, leading_rows, PREFIX_PER_SHARD, 0).astype(jnp.float32).reshape(PREFIX_PER_SHARD, KEY_HEADS, HEAD_WIDTH)
        scores = jnp.einsum('rgid,kgd->rgik', grouped_query, key_block_slice, precision=highest) * scale_factor
        block_max = lax.optimization_barrier(jnp.max(scores, axis=3))
        weights = jnp.exp(scores - block_max[..., None])
        block_den = lax.optimization_barrier(jnp.sum(weights, axis=3))
        rounded = lax.optimization_barrier(weights.astype(jnp.bfloat16)).astype(jnp.float32)
        block_num = jnp.einsum('rgik,kgd->rgid', rounded, value_block_slice, precision=highest)
        new_max = jnp.maximum(run_max, block_max)
        old_factor = jnp.exp(run_max - new_max)
        new_factor = jnp.exp(block_max - new_max)
        run_num = run_num * old_factor[..., None] + block_num * new_factor[..., None]
        run_den = run_den * old_factor + block_den * new_factor
        return ((new_max, run_num, run_den), None)
    initial_maximum = jnp.full((every_row, KEY_HEADS, queries_per_group), negative_fill, jnp.float32)
    initial_numerator = jnp.zeros((every_row, KEY_HEADS, queries_per_group, HEAD_WIDTH), jnp.float32)
    initial_denominator = jnp.zeros((every_row, KEY_HEADS, queries_per_group), jnp.float32)
    (pref_max, pref_num, pref_den), unused = lax.scan(block_step, (initial_maximum, initial_numerator, initial_denominator), jnp.arange(N_CTX, dtype=jnp.int32))
    closure = ancestors(parents)
    tree_query = grouped_query.reshape(DRAFT_TREES, TREE_NODES, KEY_HEADS, queries_per_group, HEAD_WIDTH)
    tree_key_rows = tree_key_heads.astype(jnp.float32).reshape(DRAFT_TREES, TREE_NODES, KEY_HEADS, HEAD_WIDTH)
    tree_value_rows = tree_value_heads.astype(jnp.float32).reshape(DRAFT_TREES, TREE_NODES, KEY_HEADS, HEAD_WIDTH)
    tree_scores = jnp.einsum('tngid,tjgd->tngij', tree_query, tree_key_rows, precision=highest) * scale_factor
    tree_scores = jnp.where(closure[:, :, None, None, :] > 0.5, tree_scores, negative_fill)
    tree_maximum = lax.optimization_barrier(jnp.max(tree_scores, axis=4))
    tree_weights = jnp.exp(tree_scores - tree_maximum[..., None])
    tree_denominator = lax.optimization_barrier(jnp.sum(tree_weights, axis=4))
    rounded_tree = lax.optimization_barrier(tree_weights.astype(jnp.bfloat16)).astype(jnp.float32)
    tree_numerator = jnp.einsum('tngij,tjgd->tngid', rounded_tree, tree_value_rows, precision=highest)
    tree_maximum = tree_maximum.reshape(every_row, KEY_HEADS, queries_per_group)
    tree_denominator = tree_denominator.reshape(every_row, KEY_HEADS, queries_per_group)
    tree_numerator = tree_numerator.reshape(every_row, KEY_HEADS, queries_per_group, HEAD_WIDTH)
    final_max = jnp.maximum(pref_max, tree_maximum)
    pref_scale = jnp.exp(pref_max - final_max)
    tree_scale = jnp.exp(tree_maximum - final_max)
    numer = pref_num * pref_scale[..., None] + tree_numerator * tree_scale[..., None]
    denom = pref_den * pref_scale + tree_denominator * tree_scale
    attended = (numer / denom[..., None]).reshape(every_row, QUERY_HEADS * HEAD_WIDTH).astype(jnp.bfloat16)
    joined = jnp.dot(token_embed, fc_embed, preferred_element_type=jnp.float32) + jnp.dot(attended, fc_feature, preferred_element_type=jnp.float32)
    mean_square = lax.optimization_barrier(jnp.mean(joined * joined, axis=1, keepdims=True))
    normed = joined * lax.rsqrt(mean_square + 1e-06) * draft_gain[None, :]
    on_path = path_rows(closure, accepted).reshape(every_row, 1)
    draft_input = jnp.where(on_path > 0.5, normed, 0.0).astype(jnp.bfloat16)
    return (attended, draft_input)
```

```python
import functools
import math

import jax
import jax.numpy as jnp
from jax import lax
from jax.experimental import pallas as pl
from jax.experimental.pallas import tpu as pltpu
from jax.sharding import PartitionSpec as P

QUERY_HEADS = 64
KEY_HEADS = 8
HEAD_WIDTH = 128
PER_KEY = QUERY_HEADS // KEY_HEADS
SLOTS = 8
LANES = 128
GROUP = KEY_HEADS
HEAD_COLUMNS = PER_KEY * HEAD_WIDTH
WEIGHT_PIECES = 4
NEGATIVE = -1e30
LOG2_SCALE = HEAD_WIDTH**-0.5 * math.log2(math.e)

f32 = jnp.float32
bf16 = jnp.bfloat16


def dot_t(a, b):
    return lax.dot_general(a, b, (((1,), (1,)), ((), ())), preferred_element_type=f32)


def dot(a, b):
    return lax.dot_general(a, b, (((1,), (0,)), ((), ())), preferred_element_type=f32)


def attend(q, slabs, positions, tree_kv, bias):
    scores = [dot_t(q, s[0:positions, 0:HEAD_WIDTH]) for s in slabs]
    scores.append(dot_t(q, tree_kv[:, 0:HEAD_WIDTH]) + bias)
    top = scores[-1].max(axis=1, keepdims=True)
    for s in scores[:-1]:
        top = jnp.maximum(top, s.max(axis=1, keepdims=True))
    den = jnp.zeros_like(top)
    num = jnp.zeros((q.shape[0], HEAD_WIDTH), f32)
    values = [s[0:positions, HEAD_WIDTH : 2 * HEAD_WIDTH] for s in slabs]
    values.append(tree_kv[:, HEAD_WIDTH : 2 * HEAD_WIDTH])
    for s, v in zip(scores, values):
        w = jnp.exp2((s - top) * LOG2_SCALE)
        den = den + w.sum(axis=1, keepdims=True)
        num = num + dot(w.astype(bf16), v)
    return num / den, top * LOG2_SCALE + jnp.log2(den)


def stack_heads(q):
    q = q.astype(f32)
    return jnp.concatenate(
        [q[:, h * HEAD_WIDTH : (h + 1) * HEAD_WIDTH] for h in range(PER_KEY)], axis=0
    ).astype(bf16)


def bulk_kernel(place_ref, mix_ref, *refs, planes, positions):
    slabs = refs[:GROUP]
    tree_ref, bias_ref = refs[GROUP : GROUP + 2]
    outs = refs[GROUP + 2 :]
    rows = outs[0].shape[0]
    for p in range(planes):
        start = pl.multiple_of((place_ref[0] ^ p) * rows, rows)
        q_rows = mix_ref[pl.ds(start, rows), 0:HEAD_COLUMNS]
        bias_rows = bias_ref[pl.ds(start, rows), :]
        step = min(rows, 32)
        for first in range(0, rows, step):
            piece = slice(first, first + step)
            q = stack_heads(q_rows[piece])
            bias = jnp.concatenate([bias_rows[piece]] * PER_KEY, axis=0)
            out, lse = attend(q, slabs, positions, tree_ref, bias)
            lane = lax.broadcasted_iota(jnp.int32, (step, LANES), 1)
            stats = jnp.zeros((step, LANES), f32)
            for h in range(PER_KEY):
                part = slice(h * step, (h + 1) * step)
                column = slice(h * HEAD_WIDTH, (h + 1) * HEAD_WIDTH)
                outs[p][piece, column] = out[part].astype(bf16)
                high = lse[part].astype(bf16).astype(f32)
                middle = (lse[part] - high).astype(bf16).astype(f32)
                low = lse[part] - high - middle
                stats = jnp.where(lane == h, high, stats)
                stats = jnp.where(lane == PER_KEY + h, middle, stats)
                stats = jnp.where(lane == 2 * PER_KEY + h, low, stats)
            outs[p][piece, HEAD_COLUMNS : HEAD_COLUMNS + LANES] = stats.astype(bf16)


def accepted_kernel(place_ref, mix_ref, *refs, planes, positions, feat):
    slabs = refs[:GROUP]
    tree_ref, bias_ref, pick_ref = refs[GROUP : GROUP + 3]
    outs = refs[GROUP + 3 : GROUP + 3 + planes]
    hold_ref = refs[GROUP + 3 + planes]
    rows = pick_ref.shape[0]
    q = stack_heads(dot(pick_ref[...], mix_ref[:, 0:HEAD_COLUMNS]))
    bias = jnp.concatenate([bias_ref[...]] * PER_KEY, axis=0)
    out, lse = attend(q, slabs, positions, tree_ref, bias)
    lane = lax.broadcasted_iota(jnp.int32, (rows, LANES), 1)
    stats = [jnp.zeros((rows, LANES), f32) for _ in range(planes)]
    for h in range(PER_KEY):
        chunk, start = h * HEAD_WIDTH // feat, h * HEAD_WIDTH % feat
        part = slice(h * rows, (h + 1) * rows)
        hold_ref[chunk, :, start : start + HEAD_WIDTH] = out[part]
        stats[chunk] = jnp.where(lane == start // HEAD_WIDTH, lse[part], stats[chunk])
    for chunk in range(planes):
        hold_ref[chunk, :, feat : feat + LANES] = stats[chunk]
    for k in range(planes):
        outs[k][...] = hold_ref[place_ref[0] ^ k]


def merge_head(parts, logs):
    top = functools.reduce(jnp.maximum, logs)
    weights = [jnp.exp2(s - top) for s in logs]
    den = functools.reduce(jnp.add, weights)
    num = functools.reduce(jnp.add, [w * p for w, p in zip(weights, parts)])
    return num / den


def merge_kernel(*refs):
    mine, out_ref = refs[:-1], refs[-1]
    devices, owned, _ = out_ref.shape
    stats = [m[:, HEAD_COLUMNS : HEAD_COLUMNS + LANES].astype(f32) for m in mine]
    for h in range(PER_KEY):
        logs = [
            s[:, h : h + 1]
            + s[:, PER_KEY + h : PER_KEY + h + 1]
            + s[:, 2 * PER_KEY + h : 2 * PER_KEY + h + 1]
            for s in stats
        ]
        column = slice(h * HEAD_WIDTH, (h + 1) * HEAD_WIDTH)
        merged = merge_head([m[:, column].astype(f32) for m in mine], logs)
        out_ref[:, :, column] = merged.reshape(devices, owned, HEAD_WIDTH).astype(bf16)


def mix_kernel(query_ref, embed_ref, out_ref, *, key_of):
    size = out_ref.shape[0]
    feat = embed_ref.shape[1] // size
    for d in range(size):
        start = key_of[d % GROUP] * HEAD_COLUMNS
        out_ref[d, :, 0:HEAD_COLUMNS] = query_ref[:, start : start + HEAD_COLUMNS]
        out_ref[d, :, HEAD_COLUMNS : HEAD_COLUMNS + feat] = embed_ref[:, d * feat : (d + 1) * feat]


def embed_kernel(pick_ref, mix_ref, *refs):
    weights, out_ref = refs[:-1], refs[-1]
    rows = dot(pick_ref[...], mix_ref[:, HEAD_COLUMNS:]).astype(bf16)
    depth = weights[0].shape[0]
    total = dot(rows[:, 0:depth], weights[0][...])
    for i, w in enumerate(weights[1:], 1):
        total = total + dot(rows[:, i * depth : (i + 1) * depth], w[...])
    out_ref[...] = total.reshape(out_ref.shape)


def feature_kernel(*refs, planes, feat):
    messages = refs[:planes]
    weights = refs[planes : planes + WEIGHT_PIECES]
    add_ref, out_ref, rows_ref = refs[planes + WEIGHT_PIECES :]

    @pl.when(pl.program_id(0) == 0)
    def _():
        for h in range(feat // HEAD_WIDTH):
            column = slice(h * HEAD_WIDTH, (h + 1) * HEAD_WIDTH)
            merged = merge_head(
                [m[:, column] for m in messages],
                [m[:, feat + h : feat + h + 1] for m in messages],
            )
            rows_ref[:, column] = merged.astype(bf16)

    depth = feat // WEIGHT_PIECES
    total = dot(rows_ref[:, 0:depth], weights[0][...])
    for i in range(1, WEIGHT_PIECES):
        total = total + dot(rows_ref[:, i * depth : (i + 1) * depth], weights[i][...])
    out_ref[...] = total.reshape(out_ref.shape) + add_ref[...]


def norm_kernel(joined_ref, gain_ref, pick_ref, out_ref):
    chunks, slots, width = joined_ref.shape
    total = jnp.zeros((slots, 1), f32)
    for c in range(chunks):
        total = total + jnp.sum(joined_ref[c] * joined_ref[c], axis=1, keepdims=True)
    factor = lax.rsqrt(total / (chunks * width) + 1e-06)
    pick = pick_ref[...]
    for c in range(chunks):
        normed = joined_ref[c] * factor * gain_ref[:, c * width : (c + 1) * width]
        rows = jnp.zeros((pick.shape[0], width), f32)
        for s in range(slots):
            rows = rows + jnp.where(pick[:, s : s + 1] > 0.5, normed[s : s + 1, :], 0.0)
        out_ref[:, c * width : (c + 1) * width] = rows.astype(bf16)


def ancestors(parents):
    nodes = parents.shape[1]
    column = jnp.arange(nodes, dtype=jnp.int32)
    upward = (parents[:, :, None] == column[None, None, :]).astype(f32)
    closure = jnp.maximum(upward, jnp.eye(nodes, dtype=f32)[None])
    for repeat in range(3):
        closure = jnp.minimum(jnp.einsum("tij,tjk->tik", closure, closure), 1.0)
    return closure


def body(
    queries,
    prefix_key_heads,
    prefix_value_heads,
    tree_key_heads,
    tree_value_heads,
    token_embed,
    fc_embed,
    fc_feature,
    draft_gain,
    parents,
    accepted,
):
    size = lax.axis_size("ctx")
    me = lax.axis_index("ctx")
    trees, nodes = parents.shape
    owned, model = queries.shape
    positions = prefix_key_heads.shape[0]
    feat = fc_feature.shape[0]
    every_row = trees * nodes
    planes = size // GROUP
    plane, seat = me // GROUP, me % GROUP
    plane_rows = GROUP * owned
    chunks = size // trees
    part = model // chunks
    mixed = HEAD_COLUMNS + feat
    key_of = [(w >> 1) | ((w & 1) * (GROUP // 2)) for w in range(GROUP)]

    def key_at(w):
        return (w >> 1) | ((w & 1) * (GROUP // 2))

    def swap(x, mask):
        return lax.ppermute(x, "ctx", [(s, s ^ mask) for s in range(size)])

    plane_groups = [[p * GROUP + g for g in range(GROUP)] for p in range(planes)]
    tree_groups = [[t * chunks + c for c in range(chunks)] for t in range(trees)]

    slabs = []
    for r in range(GROUP):
        start = key_at(seat ^ r) * HEAD_WIDTH

        def take(x):
            return lax.dynamic_slice_in_dim(x, start, HEAD_WIDTH, 1)

        slab = jnp.concatenate(
            [
                jnp.concatenate([take(prefix_key_heads), take(prefix_value_heads)], axis=1),
                jnp.concatenate([take(tree_key_heads), take(tree_value_heads)], axis=1),
            ],
            axis=0,
        )
        slabs.append(swap(slab, r) if r else slab)

    packed = pl.pallas_call(
        functools.partial(mix_kernel, key_of=key_of),
        out_shape=jax.ShapeDtypeStruct((size, owned, mixed), bf16),
        name="pack",
    )(queries, token_embed)
    mix = lax.all_to_all(
        packed, "ctx", split_axis=0, concat_axis=0, tiled=True
    ).reshape(every_row, mixed)

    closure = ancestors(parents)
    chosen = (accepted[:, None] == jnp.arange(nodes, dtype=jnp.int32)[None, :]).astype(f32)
    on_path = jnp.einsum("ti,tij->tj", chosen, closure)
    upto = (jnp.arange(nodes)[:, None] <= jnp.arange(nodes)[None, :]).astype(f32)
    rank = jnp.dot(on_path, upto)
    slot = jnp.arange(1, SLOTS + 1, dtype=f32)
    pick = jnp.where(
        (rank[:, None, :] == slot[None, :, None]) & (on_path[:, None, :] > 0.5), 1.0, 0.0
    )
    same = jnp.eye(trees, dtype=f32)
    pick_rows = (same[:, None, :, None] * pick[:, :, None, :]).reshape(trees * SLOTS, every_row)
    reach = (same[:, None, :, None] * closure[:, :, None, :]).reshape(every_row, every_row)
    row = jnp.arange(every_row, dtype=jnp.int32)
    key = jnp.arange(LANES, dtype=jnp.int32)
    key_row = plane * plane_rows + (seat ^ (key // owned)) * owned + key % owned
    key_row = jnp.where(key < plane_rows, key_row, -1)
    keys_hot = (row[:, None] == key_row[None, :]).astype(f32)
    bias = jnp.where(jnp.dot(reach, keys_hot) > 0.5, 0.0, NEGATIVE)
    pick_rows = pick_rows.astype(bf16)
    bias_picked = jnp.where(jnp.dot(jnp.dot(pick_rows, reach), keys_hot) > 0.5, 0.0, NEGATIVE)
    own_tree = (jnp.arange(trees) == me // chunks).astype(f32)
    own_rows = (me * owned + jnp.arange(owned))[:, None] == row[None, :]
    own_pick = jnp.einsum(
        "rj,tsj->rs",
        own_rows.astype(f32),
        pick_rows.astype(f32).reshape(trees, SLOTS, every_row) * own_tree[:, None, None],
    )
    place = plane.astype(jnp.int32)[None]

    weight_specs = [
        pl.BlockSpec((feat // WEIGHT_PIECES, part), lambda c, i=i: (i, c))
        for i in range(WEIGHT_PIECES)
    ]
    sum_spec = pl.BlockSpec((trees, 1, SLOTS, part), lambda c: (0, c, 0, 0))
    sum_shape = jax.ShapeDtypeStruct((trees, chunks, SLOTS, part), f32)
    embed_part = pl.pallas_call(
        embed_kernel,
        grid=(chunks,),
        in_specs=[
            pl.BlockSpec((trees * SLOTS, every_row), lambda c: (0, 0)),
            pl.BlockSpec((every_row, mixed), lambda c: (0, 0)),
        ]
        + weight_specs,
        out_specs=sum_spec,
        out_shape=sum_shape,
        name="embed_join",
    )(pick_rows, mix, *[fc_embed] * WEIGHT_PIECES)

    tree_kv = jnp.concatenate([s[positions:] for s in slabs], axis=0)
    tree_kv = jnp.pad(tree_kv, ((0, LANES - plane_rows), (0, 0)))
    scalar = pl.BlockSpec(memory_space=pltpu.SMEM)
    block = pl.BlockSpec(memory_space=pltpu.VMEM)

    messages = pl.pallas_call(
        functools.partial(accepted_kernel, planes=planes, positions=positions, feat=feat),
        in_specs=[scalar] + [block] * (GROUP + 4),
        out_shape=[jax.ShapeDtypeStruct((trees * SLOTS, feat + LANES), f32)] * planes,
        scratch_shapes=[pltpu.VMEM((planes, trees * SLOTS, feat + LANES), f32)],
        name="accepted",
    )(place, mix, *slabs, tree_kv, bias_picked, pick_rows)
    arrived = [
        lax.ppermute(
            messages[k],
            "ctx",
            [
                (p * GROUP + w, planes * key_of[w] + (p ^ k))
                for p in range(planes)
                for w in range(GROUP)
            ],
        )
        for k in range(planes)
    ]
    partial_sums = pl.pallas_call(
        functools.partial(feature_kernel, planes=planes, feat=feat),
        grid=(chunks,),
        in_specs=[pl.BlockSpec((trees * SLOTS, feat + LANES), lambda c: (0, 0))] * planes
        + weight_specs
        + [sum_spec],
        out_specs=sum_spec,
        out_shape=sum_shape,
        scratch_shapes=[pltpu.VMEM((trees * SLOTS, feat), bf16)],
        name="feature_join",
    )(*arrived, *[fc_feature] * WEIGHT_PIECES, embed_part)

    pieces = lax.all_to_all(
        partial_sums.reshape(size, SLOTS, part),
        "ctx",
        split_axis=0,
        concat_axis=0,
        tiled=True,
    )
    summed = jnp.sum(pieces, axis=0)
    joined = lax.all_to_all(
        jnp.broadcast_to(summed[None], (chunks, SLOTS, part)),
        "ctx",
        split_axis=0,
        concat_axis=0,
        tiled=True,
        axis_index_groups=tree_groups,
    )
    draft_input = pl.pallas_call(
        norm_kernel,
        out_shape=jax.ShapeDtypeStruct((owned, model), bf16),
        name="norm",
    )(joined, draft_gain[None, :], own_pick)

    out = pl.pallas_call(
        functools.partial(bulk_kernel, planes=planes, positions=positions),
        in_specs=[scalar] + [block] * (GROUP + 3),
        out_shape=[jax.ShapeDtypeStruct((plane_rows, HEAD_COLUMNS + LANES), bf16)] * planes,
        name="bulk",
    )(place, mix, *slabs, tree_kv, bias)
    gathered = [out[0]] + [swap(out[p], GROUP * p) for p in range(1, planes)]
    merged = pl.pallas_call(
        merge_kernel,
        out_shape=jax.ShapeDtypeStruct((GROUP, owned, HEAD_COLUMNS), bf16),
        name="merge",
    )(*gathered)
    by_seat = lax.all_to_all(
        merged, "ctx", split_axis=0, concat_axis=0, tiled=True, axis_index_groups=plane_groups
    )
    seat_of = [key_of.index(k) for k in range(GROUP)]
    attended = jnp.concatenate([by_seat[w] for w in seat_of], axis=1)
    return (attended, draft_input)


def solution(mesh):
    placed = (
        P(("groups", "ctx"), None),
        P(("groups", "ctx"), None),
        P(("groups", "ctx"), None),
        P(("groups", "ctx"), None),
        P(("groups", "ctx"), None),
        P(("groups", "ctx"), None),
        P("ctx", None),
        P("ctx", None),
        P(),
        P("groups", None),
        P("groups"),
    )
    return jax.shard_map(
        body,
        mesh=mesh,
        in_specs=placed,
        out_specs=(P(("groups", "ctx"), None), P(("groups", "ctx"), None)),
        check_vma=False,
    )
```

```python
import functools
import math

import jax
import jax.numpy as jnp
from jax import lax
from jax.experimental import pallas as pl
from jax.experimental.pallas import tpu as pltpu
from jax.sharding import PartitionSpec as P


QUERY_HEADS = 64
KEY_HEADS = 8
HEAD_WIDTH = 128
PER_KEY = QUERY_HEADS // KEY_HEADS
SLOTS = 8
LANES = 128
GROUP = KEY_HEADS
HEAD_COLUMNS = PER_KEY * HEAD_WIDTH
WEIGHT_PIECES = 8
ROOM = 14 * 2**20
STEP = 32
ARRIVAL = (0, 2, 4, 3, 5, 6, 7, 1)
NEGATIVE = -1e30
LOG2_SCALE = HEAD_WIDTH**-0.5 * math.log2(math.e)

f32 = jnp.float32
bf16 = jnp.bfloat16


def dot_t(a, b):
    return lax.dot_general(a, b, (((1,), (1,)), ((), ())), preferred_element_type=f32)


def dot(a, b):
    return lax.dot_general(a, b, (((1,), (0,)), ((), ())), preferred_element_type=f32)


def attend(q, slabs, positions, tree_kv, bias):
    scores = [dot_t(q, s[0:positions, 0:HEAD_WIDTH]) for s in slabs]
    scores.append(dot_t(q, tree_kv[:, 0:HEAD_WIDTH]) + bias)
    top = scores[-1].max(axis=1, keepdims=True)
    for s in scores[:-1]:
        top = jnp.maximum(top, s.max(axis=1, keepdims=True))
    den = jnp.zeros_like(top)
    num = jnp.zeros((q.shape[0], HEAD_WIDTH), f32)
    values = [s[0:positions, HEAD_WIDTH : 2 * HEAD_WIDTH] for s in slabs]
    values.append(tree_kv[:, HEAD_WIDTH : 2 * HEAD_WIDTH])
    for s, v in zip(scores, values):
        w = jnp.exp2((s - top) * LOG2_SCALE)
        den = den + w.sum(axis=1, keepdims=True)
        num = num + dot(w.astype(bf16), v)
    return num / den, top * LOG2_SCALE + jnp.log2(den)


def stack_heads(q):
    q = q.astype(f32)
    return jnp.concatenate(
        [q[:, h * HEAD_WIDTH : (h + 1) * HEAD_WIDTH] for h in range(PER_KEY)], axis=0
    ).astype(bf16)


def bulk_kernel(place_ref, mix_ref, *refs, distance, first, plane_rows, positions):
    slabs = refs[:GROUP]
    tree_ref, bias_ref = refs[GROUP : GROUP + 2]
    out_ref = refs[-1]
    step = out_ref.shape[0]
    start = pl.multiple_of((place_ref[0] ^ distance) * plane_rows + first, step)
    q = stack_heads(mix_ref[pl.ds(start, step), 0:HEAD_COLUMNS])
    bias = jnp.concatenate([bias_ref[pl.ds(start, step), :]] * PER_KEY, axis=0)
    out, lse = attend(q, slabs, positions, tree_ref, bias)
    lane = lax.broadcasted_iota(jnp.int32, (step, LANES), 1)
    stats = jnp.zeros((step, LANES), f32)
    for h in range(PER_KEY):
        part = slice(h * step, (h + 1) * step)
        column = slice(h * HEAD_WIDTH, (h + 1) * HEAD_WIDTH)
        out_ref[:, column] = out[part].astype(bf16)
        high = lse[part].astype(bf16).astype(f32)
        middle = (lse[part] - high).astype(bf16).astype(f32)
        low = lse[part] - high - middle
        stats = jnp.where(lane == h, high, stats)
        stats = jnp.where(lane == PER_KEY + h, middle, stats)
        stats = jnp.where(lane == 2 * PER_KEY + h, low, stats)
    out_ref[:, HEAD_COLUMNS : HEAD_COLUMNS + LANES] = stats.astype(bf16)


def accepted_kernel(place_ref, mix_ref, *refs, planes, positions, feat):
    slabs = refs[:GROUP]
    tree_ref, bias_ref, pick_ref = refs[GROUP : GROUP + 3]
    outs = refs[GROUP + 3 : GROUP + 3 + planes]
    hold_ref = refs[GROUP + 3 + planes]
    rows = pick_ref.shape[0]
    q = stack_heads(dot(pick_ref[...], mix_ref[:, 0:HEAD_COLUMNS]))
    bias = jnp.concatenate([bias_ref[...]] * PER_KEY, axis=0)
    out, lse = attend(q, slabs, positions, tree_ref, bias)
    lane = lax.broadcasted_iota(jnp.int32, (rows, LANES), 1)
    stats = [jnp.zeros((rows, LANES), f32) for _ in range(planes)]
    for h in range(PER_KEY):
        chunk, start = h * HEAD_WIDTH // feat, h * HEAD_WIDTH % feat
        part = slice(h * rows, (h + 1) * rows)
        hold_ref[chunk, :, start : start + HEAD_WIDTH] = out[part]
        stats[chunk] = jnp.where(lane == start // HEAD_WIDTH, lse[part], stats[chunk])
    for chunk in range(planes):
        hold_ref[chunk, :, feat : feat + LANES] = stats[chunk]
    for k in range(planes):
        outs[k][...] = hold_ref[place_ref[0] ^ k]


def merge_head(parts, logs):
    top = functools.reduce(jnp.maximum, logs)
    weights = [jnp.exp2(s - top) for s in logs]
    den = functools.reduce(jnp.add, weights)
    num = functools.reduce(jnp.add, [w * p for w, p in zip(weights, parts)])
    return num / den


def merge_kernel(*refs, planes):
    out_ref = refs[-1]
    owned = out_ref.shape[1]
    for first in range(0, len(refs) - 1, planes):
        mine = refs[first : first + planes]
        rows = mine[0].shape[0]
        devices = slice(first // planes * rows // owned, (first // planes + 1) * rows // owned)
        stats = [m[:, HEAD_COLUMNS : HEAD_COLUMNS + LANES].astype(f32) for m in mine]
        for h in range(PER_KEY):
            logs = [
                s[:, h : h + 1]
                + s[:, PER_KEY + h : PER_KEY + h + 1]
                + s[:, 2 * PER_KEY + h : 2 * PER_KEY + h + 1]
                for s in stats
            ]
            column = slice(h * HEAD_WIDTH, (h + 1) * HEAD_WIDTH)
            merged = merge_head([m[:, column].astype(f32) for m in mine], logs)
            out_ref[devices, :, column] = merged.reshape(-1, owned, HEAD_WIDTH).astype(bf16)


def mix_kernel(query_ref, embed_ref, after_ref, out_ref, sems, *, key_of):
    size = out_ref.shape[0]
    feat = embed_ref.shape[1] // size
    copies = []
    for d in range(size):
        start = key_of[d % GROUP] * HEAD_COLUMNS
        pairs = (
            (query_ref.at[:, start : start + HEAD_COLUMNS], pl.ds(0, HEAD_COLUMNS)),
            (embed_ref.at[:, d * feat : (d + 1) * feat], pl.ds(HEAD_COLUMNS, feat)),
        )
        for i, (source, columns) in enumerate(pairs):
            copies.append(
                pltpu.make_async_copy(source, out_ref.at[d, :, columns], sems.at[2 * d + i])
            )
    for c in copies:
        c.start()
    for c in copies:
        c.wait()


def split_kernel(place_ref, keys_ref, values_ref, tree_keys_ref, tree_values_ref, *refs, seats):
    outs, sems = refs[-len(seats) - 1 : -1], refs[-1]
    positions, owned = keys_ref.shape[0], tree_keys_ref.shape[0]
    copies = []
    for i, r in enumerate(seats):
        seat = place_ref[1] ^ r
        head = (seat >> 1) | ((seat & 1) * (GROUP // 2))
        start = pl.multiple_of(head * HEAD_WIDTH, HEAD_WIDTH)
        for j, (x, y) in enumerate(
            ((keys_ref, tree_keys_ref), (values_ref, tree_values_ref))
        ):
            columns = pl.ds(j * HEAD_WIDTH, HEAD_WIDTH)
            for k, (source, first, rows) in enumerate(((x, 0, positions), (y, positions, owned))):
                copies.append(
                    pltpu.make_async_copy(
                        source.at[:, pl.ds(start, HEAD_WIDTH)],
                        outs[i].at[pl.ds(first, rows), columns],
                        sems.at[4 * i + 2 * j + k],
                    )
                )
    for c in copies:
        c.start()
    for c in copies:
        c.wait()


def join(rows, weight, out_ref, base_ref=None, *, trees, spots):
    _, slots, part = out_ref.shape
    chunks = len(spots) // trees
    for n in range(chunks):
        total = dot(rows, weight[:, n * part : (n + 1) * part])
        for t in range(trees):
            spot = spots[t * chunks + n]
            some = total[t * slots : (t + 1) * slots]
            out_ref[spot] = some if base_ref is None else some + base_ref[spot]


def take_halves(bit, keep_ref, send_ref, *refs):
    half = keep_ref.shape[0]
    for ref, start in ((keep_ref, bit * half), (send_ref, (1 - bit) * half)):
        parts = [r[pl.ds(start, half)] for r in refs]
        ref[...] = functools.reduce(jnp.add, parts)


def halve_kernel(bit_ref, mine_ref, other_ref, keep_ref, send_ref):
    take_halves(bit_ref[0], keep_ref, send_ref, mine_ref, other_ref)


def add_kernel(mine_ref, other_ref, out_ref):
    out_ref[...] = mine_ref[...] + other_ref[...]


def embed_kernel(pick_ref, mix_ref, weight_ref, out_ref, buffer, sems, *, trees, spots):
    depth = weight_ref.shape[0] // WEIGHT_PIECES
    copies = []
    for i in range(WEIGHT_PIECES):
        piece = pl.ds(i * depth, depth)
        copies.append(
            pltpu.make_async_copy(weight_ref.at[piece], buffer.at[piece], sems.at[i])
        )
    for c in copies:
        c.start()
    rows = dot(pick_ref[...], mix_ref[:, HEAD_COLUMNS:]).astype(bf16)
    for c in copies:
        c.wait()
    join(rows, buffer, out_ref, trees=trees, spots=spots)


def feature_kernel(bit_ref, *refs, planes, feat, trees, spots):
    messages = refs[:planes]
    weight_ref, add_ref, keep_ref, send_ref, hold_ref = refs[planes:]
    heads = []
    for h in range(feat // HEAD_WIDTH):
        column = slice(h * HEAD_WIDTH, (h + 1) * HEAD_WIDTH)
        merged = merge_head(
            [m[:, column] for m in messages],
            [m[:, feat + h : feat + h + 1] for m in messages],
        )
        heads.append(merged.astype(bf16))
    rows = heads[0] if len(heads) == 1 else jnp.concatenate(heads, axis=1)
    join(rows, weight_ref, hold_ref, add_ref, trees=trees, spots=spots)
    take_halves(bit_ref[0], keep_ref, send_ref, hold_ref)


def norm_kernel(place_ref, gain_ref, pick_ref, *refs, offsets):
    joined, out_ref = refs[:-1], refs[-1]
    chunks = len(joined)
    _, slots, width = joined[0].shape
    total = jnp.zeros((slots, width), f32)
    for x in joined:
        total = total + x[0] * x[0]
    total = jnp.sum(total, axis=1, keepdims=True)
    factor = lax.rsqrt(total / (chunks * width) + 1e-06)
    pick = pick_ref[...]
    for x, offset in zip(joined, offsets):
        columns = pl.ds(pl.multiple_of((place_ref[0] ^ offset) * width, width), width)
        normed = x[0] * factor * gain_ref[:, columns]
        rows = jnp.zeros((pick.shape[0], width), f32)
        for s in range(slots):
            rows = rows + jnp.where(pick[:, s : s + 1] > 0.5, normed[s : s + 1, :], 0.0)
        out_ref[:, columns] = rows.astype(bf16)


def ancestors(parents):
    nodes = parents.shape[1]
    column = jnp.arange(nodes, dtype=jnp.int32)
    upward = (parents[:, :, None] == column[None, None, :]).astype(f32)
    closure = jnp.maximum(upward, jnp.eye(nodes, dtype=f32)[None])
    for _ in range(3):
        closure = jnp.minimum(jnp.einsum("tij,tjk->tik", closure, closure), 1.0)
    return closure


def body(
    queries,
    prefix_key_heads,
    prefix_value_heads,
    tree_key_heads,
    tree_value_heads,
    token_embed,
    fc_embed,
    fc_feature,
    draft_gain,
    parents,
    accepted,
):
    size = lax.axis_size("ctx")
    me = lax.axis_index("ctx")
    trees, nodes = parents.shape
    owned, model = queries.shape
    positions = prefix_key_heads.shape[0]
    feat = fc_feature.shape[0]
    every_row = trees * nodes
    planes = size // GROUP
    plane, seat = me // GROUP, me % GROUP
    plane_rows = GROUP * owned
    chunks = size // trees
    part = model // chunks
    mixed = HEAD_COLUMNS + feat
    key_of = [(w >> 1) | ((w & 1) * (GROUP // 2)) for w in range(GROUP)]

    scalar = pl.BlockSpec(memory_space=pltpu.SMEM)
    block = pl.BlockSpec(memory_space=pltpu.VMEM)
    outside = pl.BlockSpec(memory_space=pl.ANY)
    stored = pl.BlockSpec(memory_space=pltpu.HBM)
    busy = pl.CostEstimate(flops=4 * 10**9, bytes_accessed=10**6, transcendentals=10**6)
    room = pltpu.CompilerParams(vmem_limit_bytes=ROOM)

    def swap(x, mask):
        return lax.ppermute(x, "ctx", [(s, s ^ mask) for s in range(size)])

    plane_groups = [[p * GROUP + g for g in range(GROUP)] for p in range(planes)]

    def leave(x):
        return pltpu.with_memory_space_constraint(x, pltpu.HBM)

    place = jnp.stack([plane, seat]).astype(jnp.int32)
    sources = [
        leave(x)
        for x in (prefix_key_heads, prefix_value_heads, tree_key_heads, tree_value_heads)
    ]

    def split(seats, after):
        return pl.pallas_call(
            functools.partial(split_kernel, seats=seats),
            in_specs=[scalar] + [stored] * 4 + [outside] * len(after),
            out_specs=[block] * len(seats),
            out_shape=[jax.ShapeDtypeStruct((positions + owned, 2 * HEAD_WIDTH), bf16)]
            * len(seats),
            scratch_shapes=[pltpu.SemaphoreType.DMA((4 * len(seats),))],
            compiler_params=room,
            name="split",
        )(place, *sources, *after)

    slabs = list(split(ARRIVAL[1:5], ()))
    slabs = list(split(ARRIVAL[:1], slabs[:1])) + slabs + list(split(ARRIVAL[5:], slabs[:1]))
    after = slabs[-1]
    for i, r in enumerate(ARRIVAL):
        if r:
            slabs[i] = swap(slabs[i], r)
    tree_kv = jnp.concatenate([s[positions:] for s in slabs], axis=0)
    tree_kv = jnp.pad(tree_kv, ((0, LANES - plane_rows), (0, 0)))
    slabs = [pltpu.with_memory_space_constraint(s, pltpu.VMEM) for s in slabs]

    packed = pl.pallas_call(
        functools.partial(mix_kernel, key_of=key_of),
        in_specs=[stored, stored, outside],
        out_specs=block,
        out_shape=jax.ShapeDtypeStruct((size, owned, mixed), bf16),
        scratch_shapes=[pltpu.SemaphoreType.DMA((2 * size,))],
        compiler_params=room,
        name="pack",
    )(leave(queries), leave(token_embed), after)
    mix = lax.all_to_all(packed, "ctx", split_axis=0, concat_axis=0, tiled=True)
    mix = pltpu.with_memory_space_constraint(mix.reshape(every_row, mixed), pltpu.VMEM)

    closure = ancestors(parents)
    chosen = (accepted[:, None] == jnp.arange(nodes, dtype=jnp.int32)[None, :]).astype(f32)
    on_path = jnp.einsum("ti,tij->tj", chosen, closure)
    upto = (jnp.arange(nodes)[:, None] <= jnp.arange(nodes)[None, :]).astype(f32)
    rank = jnp.dot(on_path, upto)
    slot = jnp.arange(1, SLOTS + 1, dtype=f32)
    pick = jnp.where(
        (rank[:, None, :] == slot[None, :, None]) & (on_path[:, None, :] > 0.5), 1.0, 0.0
    )
    same = jnp.eye(trees, dtype=f32)
    pick_rows = (same[:, None, :, None] * pick[:, :, None, :]).reshape(trees * SLOTS, every_row)
    reach = (same[:, None, :, None] * closure[:, :, None, :]).reshape(every_row, every_row)
    row = jnp.arange(every_row, dtype=jnp.int32)
    key = jnp.arange(LANES, dtype=jnp.int32)
    key_seat = seat ^ jnp.array(ARRIVAL, jnp.int32)[jnp.minimum(key // owned, GROUP - 1)]
    key_row = plane * plane_rows + key_seat * owned + key % owned
    key_row = jnp.where(key < plane_rows, key_row, -1)
    keys_hot = (row[:, None] == key_row[None, :]).astype(f32)
    bias = jnp.where(jnp.dot(reach, keys_hot) > 0.5, 0.0, NEGATIVE)
    pick_rows = pick_rows.astype(bf16)
    bias_picked = jnp.where(jnp.dot(jnp.dot(pick_rows, reach), keys_hot) > 0.5, 0.0, NEGATIVE)
    own_tree = (jnp.arange(trees) == me // chunks).astype(f32)
    own_rows = (me * owned + jnp.arange(owned))[:, None] == row[None, :]
    own_pick = jnp.einsum(
        "rj,tsj->rs",
        own_rows.astype(f32),
        pick_rows.astype(f32).reshape(trees, SLOTS, every_row) * own_tree[:, None, None],
    )

    bits = size.bit_length() - 1
    inner = chunks.bit_length() - 1
    order = [0, *range(inner, bits), *range(1, inner)]
    spots = tuple(
        sum(((d >> bit) & 1) << (bits - 1 - i) for i, bit in enumerate(order))
        for d in range(size)
    )

    def sums(devices):
        return jax.ShapeDtypeStruct((devices, SLOTS, part), f32)

    def bit_of(i):
        return ((me >> order[i]) & 1).astype(jnp.int32)[None]

    embed_part = pl.pallas_call(
        functools.partial(embed_kernel, trees=trees, spots=spots),
        in_specs=[block, block, stored],
        out_specs=block,
        out_shape=sums(size),
        scratch_shapes=[
            pltpu.VMEM((feat, model), bf16),
            pltpu.SemaphoreType.DMA((WEIGHT_PIECES,)),
        ],
        compiler_params=room,
        cost_estimate=busy,
        name="embed_join",
    )(pick_rows, mix, leave(fc_embed))

    messages = pl.pallas_call(
        functools.partial(accepted_kernel, planes=planes, positions=positions, feat=feat),
        in_specs=[scalar] + [block] * (GROUP + 4),
        out_specs=[block] * planes,
        out_shape=[jax.ShapeDtypeStruct((trees * SLOTS, feat + LANES), f32)] * planes,
        scratch_shapes=[pltpu.VMEM((planes, trees * SLOTS, feat + LANES), f32)],
        compiler_params=room,
        cost_estimate=busy,
        name="accepted",
    )(place, mix, *slabs, tree_kv, bias_picked, pick_rows)
    arrived = []
    for k in range(planes):
        target = [
            (p * GROUP + w, planes * key_of[w] + (p ^ k))
            for p in range(planes)
            for w in range(GROUP)
        ]
        arrived.append(lax.ppermute(messages[k], "ctx", target))
    arrived = [pltpu.with_memory_space_constraint(x, pltpu.VMEM) for x in arrived]
    keep, send = pl.pallas_call(
        functools.partial(feature_kernel, planes=planes, feat=feat, trees=trees, spots=spots),
        in_specs=[scalar] + [block] * (planes + 2),
        out_specs=[block] * 2,
        out_shape=[sums(size // 2)] * 2,
        scratch_shapes=[pltpu.VMEM((size, SLOTS, part), f32)],
        compiler_params=room,
        name="feature_join",
    )(bit_of(0), *arrived, fc_feature, embed_part)
    for i, bit in enumerate(order):
        other = swap(send, 1 << bit)
        other = pltpu.with_memory_space_constraint(other, pltpu.VMEM)
        if i + 1 < bits:
            keep, send = pl.pallas_call(
                halve_kernel,
                in_specs=[scalar] + [block] * 2,
                out_specs=[block] * 2,
                out_shape=[sums(size >> (i + 2))] * 2,
                compiler_params=room,
                name="halve",
            )(bit_of(i + 1), keep, other)
        else:
            own = pl.pallas_call(
                add_kernel,
                in_specs=[block] * 2,
                out_specs=block,
                out_shape=sums(1),
                compiler_params=room,
                name="add",
            )(keep, other)
    joined = [own]
    offsets = [0]
    for bit in reversed(range(inner)):
        joined = joined + [swap(x, 1 << bit) for x in joined]
        offsets = offsets + [o ^ (1 << bit) for o in offsets]
    joined = [pltpu.with_memory_space_constraint(x, pltpu.VMEM) for x in joined]
    draft_input = pl.pallas_call(
        functools.partial(norm_kernel, offsets=tuple(offsets)),
        in_specs=[scalar] + [block] * (chunks + 2),
        out_specs=block,
        out_shape=jax.ShapeDtypeStruct((owned, model), bf16),
        compiler_params=room,
        name="norm",
    )((me % chunks).astype(jnp.int32)[None], draft_gain[None, :], own_pick, *joined)

    rows = min(plane_rows, STEP)
    pieces = [(p, f) for p in [*range(1, planes), 0] for f in range(0, plane_rows, rows)]
    gathered = {}
    for p, first in pieces:
        out = pl.pallas_call(
            functools.partial(
                bulk_kernel,
                distance=p,
                first=first,
                plane_rows=plane_rows,
                positions=positions,
            ),
            in_specs=[scalar] + [block] * (GROUP + 3) + [outside],
            out_specs=block,
            out_shape=jax.ShapeDtypeStruct((rows, HEAD_COLUMNS + LANES), bf16),
            compiler_params=room,
            cost_estimate=busy,
        )(place, mix, *slabs, tree_kv, bias, messages[0])
        if p:
            out = swap(out, GROUP * p)
        gathered[first, p] = pltpu.with_memory_space_constraint(out, pltpu.VMEM)
    merged = pl.pallas_call(
        functools.partial(merge_kernel, planes=planes),
        in_specs=[block] * len(pieces),
        out_specs=block,
        out_shape=jax.ShapeDtypeStruct((GROUP, owned, HEAD_COLUMNS), bf16),
        compiler_params=room,
        name="merge",
    )(*[gathered[k] for k in sorted(gathered)])
    by_seat = lax.all_to_all(
        merged,
        "ctx",
        split_axis=0,
        concat_axis=0,
        tiled=True,
        axis_index_groups=plane_groups,
    )
    seat_of = [key_of.index(k) for k in range(GROUP)]
    attended = jnp.concatenate([by_seat[w] for w in seat_of], axis=1)
    return (attended, draft_input)


def solution(mesh):
    placed = (
        P(("groups", "ctx"), None),
        P(("groups", "ctx"), None),
        P(("groups", "ctx"), None),
        P(("groups", "ctx"), None),
        P(("groups", "ctx"), None),
        P(("groups", "ctx"), None),
        P("ctx", None),
        P("ctx", None),
        P(),
        P("groups", None),
        P("groups"),
    )
    return jax.shard_map(
        body,
        mesh=mesh,
        in_specs=placed,
        out_specs=(P(("groups", "ctx"), None), P(("groups", "ctx"), None)),
        check_vma=False,
    )
```

```python
import functools
import math

import jax
import jax.numpy as jnp
from jax import lax
from jax.experimental import pallas as pl
from jax.experimental.pallas import tpu as pltpu
from jax.sharding import PartitionSpec as P


QUERY_HEADS = 64
KEY_HEADS = 8
HEAD_WIDTH = 128
PER_KEY = QUERY_HEADS // KEY_HEADS
SLOTS = 8
LANES = 128
GROUP = KEY_HEADS
HEAD_COLUMNS = PER_KEY * HEAD_WIDTH
DIRECT = 8
ROOM = 14 * 2**20
STEP = 32
ARRIVAL = (0, 2, 4, 3, 5, 6, 7, 1)
NEGATIVE = -1e30
LOG2_SCALE = HEAD_WIDTH**-0.5 * math.log2(math.e)

f32 = jnp.float32
bf16 = jnp.bfloat16


def dot_t(a, b):
    return lax.dot_general(a, b, (((1,), (1,)), ((), ())), preferred_element_type=f32)


def dot(a, b):
    return lax.dot_general(a, b, (((1,), (0,)), ((), ())), preferred_element_type=f32)


def attend(q, slabs, positions, tree_kv, bias):
    scores = [dot_t(q, s[0:positions, 0:HEAD_WIDTH]) for s in slabs]
    scores.append(dot_t(q, tree_kv[:, 0:HEAD_WIDTH]) + bias)
    top = scores[-1].max(axis=1, keepdims=True)
    for s in scores[:-1]:
        top = jnp.maximum(top, s.max(axis=1, keepdims=True))
    den = jnp.zeros_like(top)
    num = jnp.zeros((q.shape[0], HEAD_WIDTH), f32)
    values = [s[0:positions, HEAD_WIDTH : 2 * HEAD_WIDTH] for s in slabs]
    values.append(tree_kv[:, HEAD_WIDTH : 2 * HEAD_WIDTH])
    for s, v in zip(scores, values):
        w = jnp.exp2((s - top) * LOG2_SCALE)
        den = den + w.sum(axis=1, keepdims=True)
        num = num + dot(w.astype(bf16), v)
    return num / den, top * LOG2_SCALE + jnp.log2(den)


def stack_heads(q):
    q = q.astype(f32)
    return jnp.concatenate(
        [q[:, h * HEAD_WIDTH : (h + 1) * HEAD_WIDTH] for h in range(PER_KEY)], axis=0
    ).astype(bf16)


def bulk_kernel(place_ref, mix_ref, *refs, distance, first, plane_rows, positions):
    slabs = refs[:GROUP]
    tree_ref, bias_ref = refs[GROUP : GROUP + 2]
    out_ref = refs[-1]
    step = out_ref.shape[0]
    start = pl.multiple_of((place_ref[0] ^ distance) * plane_rows + first, step)
    q = stack_heads(mix_ref[pl.ds(start, step), 0:HEAD_COLUMNS])
    bias = jnp.concatenate([bias_ref[pl.ds(start, step), :]] * PER_KEY, axis=0)
    out, lse = attend(q, slabs, positions, tree_ref, bias)
    lane = lax.broadcasted_iota(jnp.int32, (step, LANES), 1)
    stats = jnp.zeros((step, LANES), f32)
    for h in range(PER_KEY):
        part = slice(h * step, (h + 1) * step)
        column = slice(h * HEAD_WIDTH, (h + 1) * HEAD_WIDTH)
        out_ref[:, column] = out[part].astype(bf16)
        high = lse[part].astype(bf16).astype(f32)
        middle = (lse[part] - high).astype(bf16).astype(f32)
        low = lse[part] - high - middle
        stats = jnp.where(lane == h, high, stats)
        stats = jnp.where(lane == PER_KEY + h, middle, stats)
        stats = jnp.where(lane == 2 * PER_KEY + h, low, stats)
    out_ref[:, HEAD_COLUMNS : HEAD_COLUMNS + LANES] = stats.astype(bf16)


def accepted_kernel(place_ref, mix_ref, *refs, planes, positions, feat):
    slabs = refs[:GROUP]
    tree_ref, bias_ref, pick_ref = refs[GROUP : GROUP + 3]
    outs = refs[GROUP + 3 : GROUP + 3 + planes]
    hold_ref = refs[GROUP + 3 + planes]
    rows = pick_ref.shape[0]
    q = stack_heads(dot(pick_ref[...], mix_ref[:, 0:HEAD_COLUMNS]))
    bias = jnp.concatenate([bias_ref[...]] * PER_KEY, axis=0)
    out, lse = attend(q, slabs, positions, tree_ref, bias)
    lane = lax.broadcasted_iota(jnp.int32, (rows, LANES), 1)
    stats = [jnp.zeros((rows, LANES), f32) for _ in range(planes)]
    for h in range(PER_KEY):
        chunk, start = h * HEAD_WIDTH // feat, h * HEAD_WIDTH % feat
        part = slice(h * rows, (h + 1) * rows)
        hold_ref[chunk, :, start : start + HEAD_WIDTH] = out[part]
        stats[chunk] = jnp.where(lane == start // HEAD_WIDTH, lse[part], stats[chunk])
    for chunk in range(planes):
        hold_ref[chunk, :, feat : feat + LANES] = stats[chunk]
    for k in range(planes):
        outs[k][...] = hold_ref[place_ref[0] ^ k]


def merge_head(parts, logs):
    top = functools.reduce(jnp.maximum, logs)
    weights = [jnp.exp2(s - top) for s in logs]
    den = functools.reduce(jnp.add, weights)
    num = functools.reduce(jnp.add, [w * p for w, p in zip(weights, parts)])
    return num / den


def merge_kernel(*refs, planes):
    out_ref = refs[-1]
    owned = out_ref.shape[1]
    for first in range(0, len(refs) - 1, planes):
        mine = refs[first : first + planes]
        rows = mine[0].shape[0]
        devices = slice(first // planes * rows // owned, (first // planes + 1) * rows // owned)
        stats = [m[:, HEAD_COLUMNS : HEAD_COLUMNS + LANES].astype(f32) for m in mine]
        for h in range(PER_KEY):
            logs = [
                s[:, h : h + 1]
                + s[:, PER_KEY + h : PER_KEY + h + 1]
                + s[:, 2 * PER_KEY + h : 2 * PER_KEY + h + 1]
                for s in stats
            ]
            column = slice(h * HEAD_WIDTH, (h + 1) * HEAD_WIDTH)
            merged = merge_head([m[:, column].astype(f32) for m in mine], logs)
            out_ref[devices, :, column] = merged.reshape(-1, owned, HEAD_WIDTH).astype(bf16)


def mix_kernel(query_ref, embed_ref, after_ref, out_ref, sems, *, key_of):
    size = out_ref.shape[0]
    feat = embed_ref.shape[1] // size
    copies = []
    for d in range(size):
        start = key_of[d % GROUP] * HEAD_COLUMNS
        pairs = (
            (query_ref.at[:, start : start + HEAD_COLUMNS], pl.ds(0, HEAD_COLUMNS)),
            (embed_ref.at[:, d * feat : (d + 1) * feat], pl.ds(HEAD_COLUMNS, feat)),
        )
        for i, (source, columns) in enumerate(pairs):
            copies.append(
                pltpu.make_async_copy(source, out_ref.at[d, :, columns], sems.at[2 * d + i])
            )
    for c in copies:
        c.start()
    for c in copies:
        c.wait()


def split_kernel(place_ref, keys_ref, values_ref, tree_keys_ref, tree_values_ref, *refs, seats):
    outs, sems = refs[-len(seats) - 1 : -1], refs[-1]
    positions, owned = keys_ref.shape[0], tree_keys_ref.shape[0]
    copies = []
    for i, r in enumerate(seats):
        seat = place_ref[1] ^ r
        head = (seat >> 1) | ((seat & 1) * (GROUP // 2))
        start = pl.multiple_of(head * HEAD_WIDTH, HEAD_WIDTH)
        for j, (x, y) in enumerate(
            ((keys_ref, tree_keys_ref), (values_ref, tree_values_ref))
        ):
            columns = pl.ds(j * HEAD_WIDTH, HEAD_WIDTH)
            for k, (source, first, rows) in enumerate(((x, 0, positions), (y, positions, owned))):
                copies.append(
                    pltpu.make_async_copy(
                        source.at[:, pl.ds(start, HEAD_WIDTH)],
                        outs[i].at[pl.ds(first, rows), columns],
                        sems.at[4 * i + 2 * j + k],
                    )
                )
    for c in copies:
        c.start()
    for c in copies:
        c.wait()


def join(rows, weight, out_ref, base_ref=None, *, trees, spots):
    _, slots, part = out_ref.shape
    chunks = len(spots) // trees
    for n in range(chunks):
        total = dot(rows, weight[:, n * part : (n + 1) * part])
        for t in range(trees):
            spot = spots[t * chunks + n]
            some = total[t * slots : (t + 1) * slots]
            out_ref[spot] = some if base_ref is None else some + base_ref[spot]


def take_halves(bit, keep_ref, send_ref, *refs):
    half = keep_ref.shape[0]
    for ref, start in ((keep_ref, bit * half), (send_ref, (1 - bit) * half)):
        parts = [r[pl.ds(start, half)] for r in refs]
        ref[...] = functools.reduce(jnp.add, parts)


def halve_kernel(bit_ref, mine_ref, other_ref, keep_ref, send_ref):
    take_halves(bit_ref[0], keep_ref, send_ref, mine_ref, other_ref)


def add_kernel(mine_ref, other_ref, out_ref):
    out_ref[...] = mine_ref[...] + other_ref[...]


def embed_kernel(pick_ref, mix_ref, weight_ref, out_ref, *, trees, spots):
    rows = dot(pick_ref[...], mix_ref[:, HEAD_COLUMNS:]).astype(bf16)
    join(rows, weight_ref, out_ref, trees=trees, spots=spots)


def feature_kernel(bit_ref, *refs, planes, feat, trees, spots):
    messages = refs[:planes]
    weight_ref, add_ref, keep_ref, send_ref, hold_ref = refs[planes:]
    heads = []
    for h in range(feat // HEAD_WIDTH):
        column = slice(h * HEAD_WIDTH, (h + 1) * HEAD_WIDTH)
        merged = merge_head(
            [m[:, column] for m in messages],
            [m[:, feat + h : feat + h + 1] for m in messages],
        )
        heads.append(merged.astype(bf16))
    rows = heads[0] if len(heads) == 1 else jnp.concatenate(heads, axis=1)
    join(rows, weight_ref, hold_ref, add_ref, trees=trees, spots=spots)
    take_halves(bit_ref[0], keep_ref, send_ref, hold_ref)


def norm_kernel(place_ref, gain_ref, pick_ref, *refs, offsets):
    joined, out_ref = refs[:-1], refs[-1]
    chunks = len(joined)
    _, slots, width = joined[0].shape
    total = jnp.zeros((slots, width), f32)
    for x in joined:
        total = total + x[0] * x[0]
    total = jnp.sum(total, axis=1, keepdims=True)
    factor = lax.rsqrt(total / (chunks * width) + 1e-06)
    pick = pick_ref[...]
    for x, offset in zip(joined, offsets):
        columns = pl.ds(pl.multiple_of((place_ref[0] ^ offset) * width, width), width)
        normed = x[0] * factor * gain_ref[:, columns]
        rows = jnp.zeros((pick.shape[0], width), f32)
        for s in range(slots):
            rows = rows + jnp.where(pick[:, s : s + 1] > 0.5, normed[s : s + 1, :], 0.0)
        out_ref[:, columns] = rows.astype(bf16)


def bundle_kernel(merged_ref, mine_ref, other_ref, out_ref):
    devices, owned, _ = merged_ref.shape
    total = mine_ref[0] + other_ref[0]
    high = total.astype(bf16)
    low = (total - high.astype(f32)).astype(bf16)
    for d in range(devices):
        out_ref[d, 0:owned] = merged_ref[d]
        out_ref[d, owned : owned + SLOTS] = high
        out_ref[d, owned + SLOTS : owned + 2 * SLOTS] = low


def last_kernel(bundle_ref, gain_ref, pick_ref, attended_ref, draft_ref, *, key_of):
    devices, _, width = bundle_ref.shape
    owned = attended_ref.shape[0]
    joined = []
    total = jnp.zeros((SLOTS, width), f32)
    for d in range(devices):
        columns = slice(key_of[d] * width, (key_of[d] + 1) * width)
        attended_ref[:, columns] = bundle_ref[d, 0:owned]
        high = bundle_ref[d, owned : owned + SLOTS].astype(f32)
        low = bundle_ref[d, owned + SLOTS : owned + 2 * SLOTS].astype(f32)
        joined.append(high + low)
        total = total + joined[d] * joined[d]
    total = jnp.sum(total, axis=1, keepdims=True)
    factor = lax.rsqrt(total / (devices * width) + 1e-06)
    pick = pick_ref[...]
    for d in range(devices):
        columns = slice(d * width, (d + 1) * width)
        normed = joined[d] * factor * gain_ref[:, columns]
        rows = jnp.zeros((pick.shape[0], width), f32)
        for s in range(SLOTS):
            rows = rows + jnp.where(pick[:, s : s + 1] > 0.5, normed[s : s + 1, :], 0.0)
        draft_ref[:, columns] = rows.astype(bf16)


def ancestors(parents):
    nodes = parents.shape[1]
    column = jnp.arange(nodes, dtype=jnp.int32)
    upward = (parents[:, :, None] == column[None, None, :]).astype(f32)
    closure = jnp.maximum(upward, jnp.eye(nodes, dtype=f32)[None])
    for _ in range(3):
        closure = jnp.minimum(jnp.einsum("tij,tjk->tik", closure, closure), 1.0)
    return closure


def body(
    queries,
    prefix_key_heads,
    prefix_value_heads,
    tree_key_heads,
    tree_value_heads,
    token_embed,
    fc_embed,
    fc_feature,
    draft_gain,
    parents,
    accepted,
):
    size = lax.axis_size("ctx")
    me = lax.axis_index("ctx")
    trees, nodes = parents.shape
    owned, model = queries.shape
    positions = prefix_key_heads.shape[0]
    feat = fc_feature.shape[0]
    every_row = trees * nodes
    planes = size // GROUP
    plane, seat = me // GROUP, me % GROUP
    plane_rows = GROUP * owned
    chunks = size // trees
    part = model // chunks
    mixed = HEAD_COLUMNS + feat
    key_of = [(w >> 1) | ((w & 1) * (GROUP // 2)) for w in range(GROUP)]

    scalar = pl.BlockSpec(memory_space=pltpu.SMEM)
    block = pl.BlockSpec(memory_space=pltpu.VMEM)
    outside = pl.BlockSpec(memory_space=pl.ANY)
    stored = pl.BlockSpec(memory_space=pltpu.HBM)
    busy = pl.CostEstimate(flops=4 * 10**9, bytes_accessed=10**6, transcendentals=10**6)
    room = pltpu.CompilerParams(vmem_limit_bytes=ROOM)

    def swap(x, mask):
        return lax.ppermute(x, "ctx", [(s, s ^ mask) for s in range(size)])

    plane_groups = [[p * GROUP + g for g in range(GROUP)] for p in range(planes)]

    def leave(x):
        return pltpu.with_memory_space_constraint(x, pltpu.HBM)

    place = jnp.stack([plane, seat]).astype(jnp.int32)
    sources = [
        leave(x)
        for x in (prefix_key_heads, prefix_value_heads, tree_key_heads, tree_value_heads)
    ]

    def split(seats, after):
        return pl.pallas_call(
            functools.partial(split_kernel, seats=seats),
            in_specs=[scalar] + [stored] * 4 + [outside] * len(after),
            out_specs=[block] * len(seats),
            out_shape=[jax.ShapeDtypeStruct((positions + owned, 2 * HEAD_WIDTH), bf16)]
            * len(seats),
            scratch_shapes=[pltpu.SemaphoreType.DMA((4 * len(seats),))],
            compiler_params=room,
            cost_estimate=busy,
            name="split",
        )(place, *sources, *after)

    first = list(split(ARRIVAL[1:3], ()))
    second = list(split(ARRIVAL[3:6], first[:1]))
    packed = pl.pallas_call(
        functools.partial(mix_kernel, key_of=key_of),
        in_specs=[stored, stored, outside],
        out_specs=block,
        out_shape=jax.ShapeDtypeStruct((size, owned, mixed), bf16),
        scratch_shapes=[pltpu.SemaphoreType.DMA((2 * size,))],
        compiler_params=room,
        cost_estimate=busy,
        name="pack",
    )(leave(queries), leave(token_embed), second[0])
    mix = lax.all_to_all(packed, "ctx", split_axis=0, concat_axis=0, tiled=True)
    mix = pltpu.with_memory_space_constraint(mix.reshape(every_row, mixed), pltpu.VMEM)
    third = list(split(ARRIVAL[6:] + ARRIVAL[:1], [packed]))
    slabs = third[-1:] + first + second + third[:-1]
    for i, r in enumerate(ARRIVAL):
        if r:
            slabs[i] = swap(slabs[i], r)
    tree_kv = jnp.concatenate([s[positions:] for s in slabs], axis=0)
    tree_kv = jnp.pad(tree_kv, ((0, LANES - plane_rows), (0, 0)))
    slabs = [pltpu.with_memory_space_constraint(s, pltpu.VMEM) for s in slabs]

    closure = ancestors(parents)
    chosen = (accepted[:, None] == jnp.arange(nodes, dtype=jnp.int32)[None, :]).astype(f32)
    on_path = jnp.einsum("ti,tij->tj", chosen, closure)
    upto = (jnp.arange(nodes)[:, None] <= jnp.arange(nodes)[None, :]).astype(f32)
    rank = jnp.dot(on_path, upto)
    slot = jnp.arange(1, SLOTS + 1, dtype=f32)
    pick = jnp.where(
        (rank[:, None, :] == slot[None, :, None]) & (on_path[:, None, :] > 0.5), 1.0, 0.0
    )
    same = jnp.eye(trees, dtype=f32)
    pick_rows = (same[:, None, :, None] * pick[:, :, None, :]).reshape(trees * SLOTS, every_row)
    reach = (same[:, None, :, None] * closure[:, :, None, :]).reshape(every_row, every_row)
    row = jnp.arange(every_row, dtype=jnp.int32)
    key = jnp.arange(LANES, dtype=jnp.int32)
    key_seat = seat ^ jnp.array(ARRIVAL, jnp.int32)[jnp.minimum(key // owned, GROUP - 1)]
    key_row = plane * plane_rows + key_seat * owned + key % owned
    key_row = jnp.where(key < plane_rows, key_row, -1)
    keys_hot = (row[:, None] == key_row[None, :]).astype(f32)
    bias = jnp.where(jnp.dot(reach, keys_hot) > 0.5, 0.0, NEGATIVE)
    pick_rows = pick_rows.astype(bf16)
    bias_picked = jnp.where(jnp.dot(jnp.dot(pick_rows, reach), keys_hot) > 0.5, 0.0, NEGATIVE)
    own_tree = (jnp.arange(trees) == me // chunks).astype(f32)
    own_rows = (me * owned + jnp.arange(owned))[:, None] == row[None, :]
    own_pick = jnp.einsum(
        "rj,tsj->rs",
        own_rows.astype(f32),
        pick_rows.astype(f32).reshape(trees, SLOTS, every_row) * own_tree[:, None, None],
    )

    bits = size.bit_length() - 1
    inner = chunks.bit_length() - 1
    order = list(range(bits))
    spots = tuple(
        sum(((d >> bit) & 1) << (bits - 1 - i) for i, bit in enumerate(order))
        for d in range(size)
    )

    def sums(devices):
        return jax.ShapeDtypeStruct((devices, SLOTS, part), f32)

    def bit_of(i):
        return ((me >> order[i]) & 1).astype(jnp.int32)[None]

    embed_part = pl.pallas_call(
        functools.partial(embed_kernel, trees=trees, spots=spots),
        in_specs=[block] * 3,
        out_specs=block,
        out_shape=sums(size),
        compiler_params=room,
        cost_estimate=busy,
        name="embed_join",
    )(pick_rows, mix, fc_embed)

    messages = pl.pallas_call(
        functools.partial(accepted_kernel, planes=planes, positions=positions, feat=feat),
        in_specs=[scalar] + [block] * (GROUP + 4),
        out_specs=[block] * planes,
        out_shape=[jax.ShapeDtypeStruct((trees * SLOTS, feat + LANES), f32)] * planes,
        scratch_shapes=[pltpu.VMEM((planes, trees * SLOTS, feat + LANES), f32)],
        compiler_params=room,
        cost_estimate=busy,
        name="accepted",
    )(place, mix, *slabs, tree_kv, bias_picked, pick_rows)
    arrived = []
    for k in range(planes):
        target = [
            (p * GROUP + w, planes * key_of[w] + (p ^ k))
            for p in range(planes)
            for w in range(GROUP)
        ]
        arrived.append(lax.ppermute(messages[k], "ctx", target))
    arrived = [pltpu.with_memory_space_constraint(x, pltpu.VMEM) for x in arrived]
    keep, send = pl.pallas_call(
        functools.partial(feature_kernel, planes=planes, feat=feat, trees=trees, spots=spots),
        in_specs=[scalar] + [block] * (planes + 2),
        out_specs=[block] * 2,
        out_shape=[sums(size // 2)] * 2,
        scratch_shapes=[pltpu.VMEM((size, SLOTS, part), f32)],
        compiler_params=room,
        name="feature_join",
    )(bit_of(0), *arrived, fc_feature, embed_part)
    for i, bit in enumerate(order):
        other = swap(send, 1 << bit)
        other = pltpu.with_memory_space_constraint(other, pltpu.VMEM)
        if i + 1 < bits:
            keep, send = pl.pallas_call(
                halve_kernel,
                in_specs=[scalar] + [block] * 2,
                out_specs=[block] * 2,
                out_shape=[sums(size >> (i + 2))] * 2,
                compiler_params=room,
                name="halve",
            )(bit_of(i + 1), keep, other)
    rows = min(plane_rows, STEP)
    pieces = [(p, f) for p in [*range(1, planes), 0] for f in range(0, plane_rows, rows)]
    gathered = {}
    for p, first in pieces:
        out = pl.pallas_call(
            functools.partial(
                bulk_kernel,
                distance=p,
                first=first,
                plane_rows=plane_rows,
                positions=positions,
            ),
            in_specs=[scalar] + [block] * (GROUP + 3) + [outside],
            out_specs=block,
            out_shape=jax.ShapeDtypeStruct((rows, HEAD_COLUMNS + LANES), bf16),
            compiler_params=room,
            cost_estimate=busy,
        )(place, mix, *slabs, tree_kv, bias, messages[0])
        if p:
            out = swap(out, GROUP * p)
        gathered[first, p] = pltpu.with_memory_space_constraint(out, pltpu.VMEM)
    merged = pl.pallas_call(
        functools.partial(merge_kernel, planes=planes),
        in_specs=[block] * len(pieces),
        out_specs=block,
        out_shape=jax.ShapeDtypeStruct((GROUP, owned, HEAD_COLUMNS), bf16),
        compiler_params=room,
        name="merge",
    )(*[gathered[k] for k in sorted(gathered)])
    if chunks == GROUP:
        bundle = pl.pallas_call(
            bundle_kernel,
            in_specs=[block] * 3,
            out_specs=block,
            out_shape=jax.ShapeDtypeStruct((GROUP, owned + 2 * SLOTS, HEAD_COLUMNS), bf16),
            compiler_params=room,
            name="bundle",
        )(merged, keep, other)
        bundle = lax.all_to_all(
            bundle,
            "ctx",
            split_axis=0,
            concat_axis=0,
            tiled=True,
            axis_index_groups=plane_groups,
        )
        bundle = pltpu.with_memory_space_constraint(bundle, pltpu.VMEM)
        return tuple(
            pl.pallas_call(
                functools.partial(last_kernel, key_of=key_of),
                in_specs=[block] * 3,
                out_specs=[block] * 2,
                out_shape=[jax.ShapeDtypeStruct((owned, model), bf16)] * 2,
                compiler_params=room,
                name="last",
            )(bundle, draft_gain[None, :], own_pick)
        )

    own = pl.pallas_call(
        add_kernel,
        in_specs=[block] * 2,
        out_specs=block,
        out_shape=sums(1),
        compiler_params=room,
        name="add",
    )(keep, other)
    joined = [own]
    offsets = [0]
    masks = [(1 << bit,) for bit in reversed(range(inner)) if 1 << bit >= DIRECT]
    masks.append(tuple(range(1, min(DIRECT, chunks))))
    for mask in masks:
        joined = joined + [swap(x, m) for m in mask for x in joined]
        offsets = offsets + [o ^ m for m in mask for o in offsets]
    joined = [pltpu.with_memory_space_constraint(x, pltpu.VMEM) for x in joined]
    draft_input = pl.pallas_call(
        functools.partial(norm_kernel, offsets=tuple(offsets)),
        in_specs=[scalar] + [block] * (chunks + 2),
        out_specs=block,
        out_shape=jax.ShapeDtypeStruct((owned, model), bf16),
        compiler_params=room,
        name="norm",
    )((me % chunks).astype(jnp.int32)[None], draft_gain[None, :], own_pick, *joined)

    by_seat = lax.all_to_all(
        merged,
        "ctx",
        split_axis=0,
        concat_axis=0,
        tiled=True,
        axis_index_groups=plane_groups,
    )
    seat_of = [key_of.index(k) for k in range(GROUP)]
    attended = jnp.concatenate([by_seat[w] for w in seat_of], axis=1)
    return (attended, draft_input)


def solution(mesh):
    placed = (
        P(("groups", "ctx"), None),
        P(("groups", "ctx"), None),
        P(("groups", "ctx"), None),
        P(("groups", "ctx"), None),
        P(("groups", "ctx"), None),
        P(("groups", "ctx"), None),
        P("ctx", None),
        P("ctx", None),
        P(),
        P("groups", None),
        P("groups"),
    )
    return jax.shard_map(
        body,
        mesh=mesh,
        in_specs=placed,
        out_specs=(P(("groups", "ctx"), None), P(("groups", "ctx"), None)),
        check_vma=False,
    )
```

```python
import functools
import math

import jax
import jax.numpy as jnp
from jax import lax
from jax.experimental import pallas as pl
from jax.experimental.pallas import tpu as pltpu
from jax.sharding import PartitionSpec as P


QUERY_HEADS = 64
KEY_HEADS = 8
HEAD_WIDTH = 128
PER_KEY = QUERY_HEADS // KEY_HEADS
SLOTS = 8
LANES = 128
GROUP = KEY_HEADS
HEAD_COLUMNS = PER_KEY * HEAD_WIDTH
DIRECT = 8
ROOM = 14 * 2**20
STEP = 32
ARRIVAL = (0, 4, 2, 5, 3, 6, 7, 1)
NEGATIVE = -1e30
LOG2_SCALE = HEAD_WIDTH**-0.5 * math.log2(math.e)

f32 = jnp.float32
bf16 = jnp.bfloat16


def dot_t(a, b):
    return lax.dot_general(a, b, (((1,), (1,)), ((), ())), preferred_element_type=f32)


def dot(a, b):
    return lax.dot_general(a, b, (((1,), (0,)), ((), ())), preferred_element_type=f32)


def attend(q, slabs, positions, tree_kv, bias):
    scores = [dot_t(q, s[0:positions, 0:HEAD_WIDTH]) for s in slabs]
    scores.append(dot_t(q, tree_kv[:, 0:HEAD_WIDTH]) + bias)
    top = scores[-1].max(axis=1, keepdims=True)
    for s in scores[:-1]:
        top = jnp.maximum(top, s.max(axis=1, keepdims=True))
    den = jnp.zeros_like(top)
    num = jnp.zeros((q.shape[0], HEAD_WIDTH), f32)
    values = [s[0:positions, HEAD_WIDTH : 2 * HEAD_WIDTH] for s in slabs]
    values.append(tree_kv[:, HEAD_WIDTH : 2 * HEAD_WIDTH])
    for s, v in zip(scores, values):
        w = jnp.exp2((s - top) * LOG2_SCALE)
        den = den + w.sum(axis=1, keepdims=True)
        num = num + dot(w.astype(bf16), v)
    return num / den, top * LOG2_SCALE + jnp.log2(den)


def stack_heads(q):
    q = q.astype(f32)
    return jnp.concatenate(
        [q[:, h * HEAD_WIDTH : (h + 1) * HEAD_WIDTH] for h in range(PER_KEY)], axis=0
    ).astype(bf16)


def bulk_kernel(place_ref, mix_ref, *refs, distance, first, plane_rows, positions):
    slabs = refs[:GROUP]
    tree_ref, bias_ref = refs[GROUP : GROUP + 2]
    out_ref = refs[-1]
    rows = out_ref.shape[0]
    step = min(rows, STEP)
    for tile in range(0, rows, step):
        start = pl.multiple_of((place_ref[0] ^ distance) * plane_rows + first + tile, step)
        q = stack_heads(mix_ref[pl.ds(start, step), 0:HEAD_COLUMNS])
        bias = jnp.concatenate([bias_ref[pl.ds(start, step), :]] * PER_KEY, axis=0)
        out, lse = attend(q, slabs, positions, tree_ref, bias)
        lane = lax.broadcasted_iota(jnp.int32, (step, LANES), 1)
        stats = jnp.zeros((step, LANES), f32)
        piece = slice(tile, tile + step)
        for h in range(PER_KEY):
            part = slice(h * step, (h + 1) * step)
            column = slice(h * HEAD_WIDTH, (h + 1) * HEAD_WIDTH)
            out_ref[piece, column] = out[part].astype(bf16)
            high = lse[part].astype(bf16).astype(f32)
            middle = (lse[part] - high).astype(bf16).astype(f32)
            low = lse[part] - high - middle
            stats = jnp.where(lane == h, high, stats)
            stats = jnp.where(lane == PER_KEY + h, middle, stats)
            stats = jnp.where(lane == 2 * PER_KEY + h, low, stats)
        out_ref[piece, HEAD_COLUMNS : HEAD_COLUMNS + LANES] = stats.astype(bf16)


def accepted_kernel(place_ref, mix_ref, *refs, planes, positions, feat):
    slabs = refs[:GROUP]
    tree_ref, bias_ref, pick_ref = refs[GROUP : GROUP + 3]
    outs = refs[GROUP + 3 : GROUP + 3 + planes]
    hold_ref = refs[GROUP + 3 + planes]
    rows = pick_ref.shape[0]
    q = stack_heads(dot(pick_ref[...], mix_ref[:, 0:HEAD_COLUMNS]))
    bias = jnp.concatenate([bias_ref[...]] * PER_KEY, axis=0)
    out, lse = attend(q, slabs, positions, tree_ref, bias)
    lane = lax.broadcasted_iota(jnp.int32, (rows, LANES), 1)
    stats = [jnp.zeros((rows, LANES), f32) for _ in range(planes)]
    for h in range(PER_KEY):
        chunk, start = h * HEAD_WIDTH // feat, h * HEAD_WIDTH % feat
        part = slice(h * rows, (h + 1) * rows)
        hold_ref[chunk, :, start : start + HEAD_WIDTH] = out[part]
        stats[chunk] = jnp.where(lane == start // HEAD_WIDTH, lse[part], stats[chunk])
    for chunk in range(planes):
        hold_ref[chunk, :, feat : feat + LANES] = stats[chunk]
    for k in range(planes):
        outs[k][...] = hold_ref[place_ref[0] ^ k]


def merge_head(parts, logs):
    top = functools.reduce(jnp.maximum, logs)
    weights = [jnp.exp2(s - top) for s in logs]
    den = functools.reduce(jnp.add, weights)
    num = functools.reduce(jnp.add, [w * p for w, p in zip(weights, parts)])
    return num / den


def merge_kernel(*refs, planes):
    out_ref = refs[-1]
    owned = out_ref.shape[1]
    for first in range(0, len(refs) - 1, planes):
        mine = refs[first : first + planes]
        rows = mine[0].shape[0]
        devices = slice(first // planes * rows // owned, (first // planes + 1) * rows // owned)
        stats = [m[:, HEAD_COLUMNS : HEAD_COLUMNS + LANES].astype(f32) for m in mine]
        for h in range(PER_KEY):
            logs = [
                s[:, h : h + 1]
                + s[:, PER_KEY + h : PER_KEY + h + 1]
                + s[:, 2 * PER_KEY + h : 2 * PER_KEY + h + 1]
                for s in stats
            ]
            column = slice(h * HEAD_WIDTH, (h + 1) * HEAD_WIDTH)
            merged = merge_head([m[:, column].astype(f32) for m in mine], logs)
            out_ref[devices, :, column] = merged.reshape(-1, owned, HEAD_WIDTH).astype(bf16)


def mix_kernel(query_ref, embed_ref, after_ref, out_ref, sems, *, key_of):
    size = out_ref.shape[0]
    feat = embed_ref.shape[1] // size
    copies = []
    for d in range(size):
        start = key_of[d % GROUP] * HEAD_COLUMNS
        pairs = (
            (query_ref.at[:, start : start + HEAD_COLUMNS], pl.ds(0, HEAD_COLUMNS)),
            (embed_ref.at[:, d * feat : (d + 1) * feat], pl.ds(HEAD_COLUMNS, feat)),
        )
        for i, (source, columns) in enumerate(pairs):
            copies.append(
                pltpu.make_async_copy(source, out_ref.at[d, :, columns], sems.at[2 * d + i])
            )
    for c in copies:
        c.start()
    for c in copies:
        c.wait()


def split_kernel(place_ref, keys_ref, values_ref, tree_keys_ref, tree_values_ref, *refs, seats):
    outs, sems = refs[-len(seats) - 1 : -1], refs[-1]
    positions, owned = keys_ref.shape[0], tree_keys_ref.shape[0]
    copies = []
    for i, r in enumerate(seats):
        seat = place_ref[1] ^ r
        head = (seat >> 1) | ((seat & 1) * (GROUP // 2))
        start = pl.multiple_of(head * HEAD_WIDTH, HEAD_WIDTH)
        for j, (x, y) in enumerate(
            ((keys_ref, tree_keys_ref), (values_ref, tree_values_ref))
        ):
            columns = pl.ds(j * HEAD_WIDTH, HEAD_WIDTH)
            for k, (source, first, rows) in enumerate(((x, 0, positions), (y, positions, owned))):
                copies.append(
                    pltpu.make_async_copy(
                        source.at[:, pl.ds(start, HEAD_WIDTH)],
                        outs[i].at[pl.ds(first, rows), columns],
                        sems.at[4 * i + 2 * j + k],
                    )
                )
    for c in copies:
        c.start()
    for c in copies:
        c.wait()


def join(rows, weight, out_ref, base_ref=None, *, trees, spots):
    _, slots, part = out_ref.shape
    chunks = len(spots) // trees
    for n in range(chunks):
        total = dot(rows, weight[:, n * part : (n + 1) * part])
        for t in range(trees):
            spot = spots[t * chunks + n]
            some = total[t * slots : (t + 1) * slots]
            out_ref[spot] = some if base_ref is None else some + base_ref[spot]


def take_halves(bit, keep_ref, send_ref, *refs):
    half = keep_ref.shape[0]
    for ref, start in ((keep_ref, bit * half), (send_ref, (1 - bit) * half)):
        parts = [r[pl.ds(start, half)] for r in refs]
        ref[...] = functools.reduce(jnp.add, parts)


def halve_kernel(bit_ref, mine_ref, other_ref, keep_ref, send_ref):
    take_halves(bit_ref[0], keep_ref, send_ref, mine_ref, other_ref)


def add_kernel(mine_ref, other_ref, out_ref):
    out_ref[...] = mine_ref[...] + other_ref[...]


def embed_kernel(pick_ref, mix_ref, weight_ref, out_ref, *, trees, spots):
    rows = dot(pick_ref[...], mix_ref[:, HEAD_COLUMNS:]).astype(bf16)
    join(rows, weight_ref, out_ref, trees=trees, spots=spots)


def feature_kernel(bit_ref, *refs, planes, feat, trees, spots):
    messages = refs[:planes]
    weight_ref, add_ref, keep_ref, send_ref, hold_ref = refs[planes:]
    heads = []
    for h in range(feat // HEAD_WIDTH):
        column = slice(h * HEAD_WIDTH, (h + 1) * HEAD_WIDTH)
        merged = merge_head(
            [m[:, column] for m in messages],
            [m[:, feat + h : feat + h + 1] for m in messages],
        )
        heads.append(merged.astype(bf16))
    rows = heads[0] if len(heads) == 1 else jnp.concatenate(heads, axis=1)
    join(rows, weight_ref, hold_ref, add_ref, trees=trees, spots=spots)
    take_halves(bit_ref[0], keep_ref, send_ref, hold_ref)


def norm_kernel(place_ref, gain_ref, pick_ref, *refs, offsets):
    joined, out_ref = refs[:-1], refs[-1]
    chunks = len(joined)
    _, slots, width = joined[0].shape
    total = jnp.zeros((slots, width), f32)
    for x in joined:
        total = total + x[0] * x[0]
    total = jnp.sum(total, axis=1, keepdims=True)
    factor = lax.rsqrt(total / (chunks * width) + 1e-06)
    pick = pick_ref[...]
    for x, offset in zip(joined, offsets):
        columns = pl.ds(pl.multiple_of((place_ref[0] ^ offset) * width, width), width)
        normed = x[0] * factor * gain_ref[:, columns]
        rows = jnp.zeros((pick.shape[0], width), f32)
        for s in range(slots):
            rows = rows + jnp.where(pick[:, s : s + 1] > 0.5, normed[s : s + 1, :], 0.0)
        out_ref[:, columns] = rows.astype(bf16)


def bundle_kernel(merged_ref, mine_ref, other_ref, out_ref):
    devices, owned, _ = merged_ref.shape
    total = mine_ref[0] + other_ref[0]
    high = total.astype(bf16)
    low = (total - high.astype(f32)).astype(bf16)
    for d in range(devices):
        out_ref[d, 0:owned] = merged_ref[d]
        out_ref[d, owned : owned + SLOTS] = high
        out_ref[d, owned + SLOTS : owned + 2 * SLOTS] = low


def last_kernel(bundle_ref, gain_ref, pick_ref, attended_ref, draft_ref, *, key_of):
    devices, _, width = bundle_ref.shape
    owned = attended_ref.shape[0]
    joined = []
    total = jnp.zeros((SLOTS, width), f32)
    for d in range(devices):
        columns = slice(key_of[d] * width, (key_of[d] + 1) * width)
        attended_ref[:, columns] = bundle_ref[d, 0:owned]
        high = bundle_ref[d, owned : owned + SLOTS].astype(f32)
        low = bundle_ref[d, owned + SLOTS : owned + 2 * SLOTS].astype(f32)
        joined.append(high + low)
        total = total + joined[d] * joined[d]
    total = jnp.sum(total, axis=1, keepdims=True)
    factor = lax.rsqrt(total / (devices * width) + 1e-06)
    pick = pick_ref[...]
    for d in range(devices):
        columns = slice(d * width, (d + 1) * width)
        normed = joined[d] * factor * gain_ref[:, columns]
        rows = jnp.zeros((pick.shape[0], width), f32)
        for s in range(SLOTS):
            rows = rows + jnp.where(pick[:, s : s + 1] > 0.5, normed[s : s + 1, :], 0.0)
        draft_ref[:, columns] = rows.astype(bf16)


def ancestors(parents):
    nodes = parents.shape[1]
    column = jnp.arange(nodes, dtype=jnp.int32)
    upward = (parents[:, :, None] == column[None, None, :]).astype(f32)
    closure = jnp.maximum(upward, jnp.eye(nodes, dtype=f32)[None])
    for _ in range(3):
        closure = jnp.minimum(jnp.einsum("tij,tjk->tik", closure, closure), 1.0)
    return closure


def body(
    queries,
    prefix_key_heads,
    prefix_value_heads,
    tree_key_heads,
    tree_value_heads,
    token_embed,
    fc_embed,
    fc_feature,
    draft_gain,
    parents,
    accepted,
):
    size = lax.axis_size("ctx")
    me = lax.axis_index("ctx")
    trees, nodes = parents.shape
    owned, model = queries.shape
    positions = prefix_key_heads.shape[0]
    feat = fc_feature.shape[0]
    every_row = trees * nodes
    planes = size // GROUP
    plane, seat = me // GROUP, me % GROUP
    plane_rows = GROUP * owned
    chunks = size // trees
    part = model // chunks
    mixed = HEAD_COLUMNS + feat
    key_of = [(w >> 1) | ((w & 1) * (GROUP // 2)) for w in range(GROUP)]

    scalar = pl.BlockSpec(memory_space=pltpu.SMEM)
    block = pl.BlockSpec(memory_space=pltpu.VMEM)
    outside = pl.BlockSpec(memory_space=pl.ANY)
    stored = pl.BlockSpec(memory_space=pltpu.HBM)
    busy = pl.CostEstimate(flops=4 * 10**9, bytes_accessed=10**6, transcendentals=10**6)
    room = pltpu.CompilerParams(vmem_limit_bytes=ROOM)

    def swap(x, mask):
        return lax.ppermute(x, "ctx", [(s, s ^ mask) for s in range(size)])

    plane_groups = [[p * GROUP + g for g in range(GROUP)] for p in range(planes)]

    def leave(x):
        return pltpu.with_memory_space_constraint(x, pltpu.HBM)

    place = jnp.stack([plane, seat]).astype(jnp.int32)
    here = plane.astype(jnp.int32)[None]
    sources = [
        leave(x)
        for x in (prefix_key_heads, prefix_value_heads, tree_key_heads, tree_value_heads)
    ]

    def split(seats, after):
        return pl.pallas_call(
            functools.partial(split_kernel, seats=seats),
            in_specs=[scalar] + [stored] * 4 + [outside] * len(after),
            out_specs=[block] * len(seats),
            out_shape=[jax.ShapeDtypeStruct((positions + owned, 2 * HEAD_WIDTH), bf16)]
            * len(seats),
            scratch_shapes=[pltpu.SemaphoreType.DMA((4 * len(seats),))],
            compiler_params=room,
            cost_estimate=busy,
            name="split",
        )(place, *sources, *after)

    first = list(split(ARRIVAL[1:3], ()))
    second = list(split(ARRIVAL[3:6], first[:1]))
    packed = pl.pallas_call(
        functools.partial(mix_kernel, key_of=key_of),
        in_specs=[stored, stored, outside],
        out_specs=block,
        out_shape=jax.ShapeDtypeStruct((size, owned, mixed), bf16),
        scratch_shapes=[pltpu.SemaphoreType.DMA((2 * size,))],
        compiler_params=room,
        cost_estimate=busy,
        name="pack",
    )(leave(queries), leave(token_embed), second[0])
    mix = lax.all_to_all(packed, "ctx", split_axis=0, concat_axis=0, tiled=True)
    mix = pltpu.with_memory_space_constraint(mix.reshape(every_row, mixed), pltpu.VMEM)
    third = list(split(ARRIVAL[6:] + ARRIVAL[:1], [packed]))
    slabs = third[-1:] + first + second + third[:-1]
    for i, r in enumerate(ARRIVAL):
        if r:
            slabs[i] = swap(slabs[i], r)
    tree_kv = jnp.concatenate([s[positions:] for s in slabs], axis=0)
    tree_kv = jnp.pad(tree_kv, ((0, LANES - plane_rows), (0, 0)))
    slabs = [pltpu.with_memory_space_constraint(s, pltpu.VMEM) for s in slabs]

    closure = ancestors(parents)
    chosen = (accepted[:, None] == jnp.arange(nodes, dtype=jnp.int32)[None, :]).astype(f32)
    on_path = jnp.einsum("ti,tij->tj", chosen, closure)
    upto = (jnp.arange(nodes)[:, None] <= jnp.arange(nodes)[None, :]).astype(f32)
    rank = jnp.dot(on_path, upto)
    slot = jnp.arange(1, SLOTS + 1, dtype=f32)
    pick = jnp.where(
        (rank[:, None, :] == slot[None, :, None]) & (on_path[:, None, :] > 0.5), 1.0, 0.0
    )
    same = jnp.eye(trees, dtype=f32)
    pick_rows = (same[:, None, :, None] * pick[:, :, None, :]).reshape(trees * SLOTS, every_row)
    reach = (same[:, None, :, None] * closure[:, :, None, :]).reshape(every_row, every_row)
    row = jnp.arange(every_row, dtype=jnp.int32)
    key = jnp.arange(LANES, dtype=jnp.int32)
    key_seat = seat ^ jnp.array(ARRIVAL, jnp.int32)[jnp.minimum(key // owned, GROUP - 1)]
    key_row = plane * plane_rows + key_seat * owned + key % owned
    key_row = jnp.where(key < plane_rows, key_row, -1)
    keys_hot = (row[:, None] == key_row[None, :]).astype(f32)
    bias = jnp.where(jnp.dot(reach, keys_hot) > 0.5, 0.0, NEGATIVE)
    pick_rows = pick_rows.astype(bf16)
    bias_picked = jnp.where(jnp.dot(jnp.dot(pick_rows, reach), keys_hot) > 0.5, 0.0, NEGATIVE)
    own_tree = (jnp.arange(trees) == me // chunks).astype(f32)
    own_rows = (me * owned + jnp.arange(owned))[:, None] == row[None, :]
    own_pick = jnp.einsum(
        "rj,tsj->rs",
        own_rows.astype(f32),
        pick_rows.astype(f32).reshape(trees, SLOTS, every_row) * own_tree[:, None, None],
    )

    bits = size.bit_length() - 1
    inner = chunks.bit_length() - 1
    order = list(range(bits))
    spots = tuple(
        sum(((d >> bit) & 1) << (bits - 1 - i) for i, bit in enumerate(order))
        for d in range(size)
    )

    def sums(devices):
        return jax.ShapeDtypeStruct((devices, SLOTS, part), f32)

    def bit_of(i):
        return ((me >> order[i]) & 1).astype(jnp.int32)[None]

    embed_part = pl.pallas_call(
        functools.partial(embed_kernel, trees=trees, spots=spots),
        in_specs=[block] * 3,
        out_specs=block,
        out_shape=sums(size),
        compiler_params=room,
        cost_estimate=busy,
        name="embed_join",
    )(pick_rows, mix, fc_embed)

    messages = pl.pallas_call(
        functools.partial(accepted_kernel, planes=planes, positions=positions, feat=feat),
        in_specs=[scalar] + [block] * (GROUP + 4),
        out_specs=[block] * planes,
        out_shape=[jax.ShapeDtypeStruct((trees * SLOTS, feat + LANES), f32)] * planes,
        scratch_shapes=[pltpu.VMEM((planes, trees * SLOTS, feat + LANES), f32)],
        compiler_params=room,
        cost_estimate=busy,
        name="accepted",
    )(here, mix, *slabs, tree_kv, bias_picked, pick_rows)
    arrived = []
    for k in range(planes):
        target = [
            (p * GROUP + w, planes * key_of[w] + (p ^ k))
            for p in range(planes)
            for w in range(GROUP)
        ]
        arrived.append(lax.ppermute(messages[k], "ctx", target))
    arrived = [pltpu.with_memory_space_constraint(x, pltpu.VMEM) for x in arrived]
    keep, send = pl.pallas_call(
        functools.partial(feature_kernel, planes=planes, feat=feat, trees=trees, spots=spots),
        in_specs=[scalar] + [block] * (planes + 2),
        out_specs=[block] * 2,
        out_shape=[sums(size // 2)] * 2,
        scratch_shapes=[pltpu.VMEM((size, SLOTS, part), f32)],
        compiler_params=room,
        name="feature_join",
    )(bit_of(0), *arrived, fc_feature, embed_part)
    for i, bit in enumerate(order):
        other = swap(send, 1 << bit)
        other = pltpu.with_memory_space_constraint(other, pltpu.VMEM)
        if i + 1 < bits:
            keep, send = pl.pallas_call(
                halve_kernel,
                in_specs=[scalar] + [block] * 2,
                out_specs=[block] * 2,
                out_shape=[sums(size >> (i + 2))] * 2,
                compiler_params=room,
                name="halve",
            )(bit_of(i + 1), keep, other)
    rows = min(plane_rows, STEP)
    pieces = [(p, f) for p in [*range(1, planes), 0] for f in range(0, plane_rows, rows)]
    gathered = {}
    for p, first in pieces:
        out = pl.pallas_call(
            functools.partial(
                bulk_kernel,
                distance=p,
                first=first,
                plane_rows=plane_rows,
                positions=positions,
            ),
            in_specs=[scalar] + [block] * (GROUP + 3) + [outside],
            out_specs=block,
            out_shape=jax.ShapeDtypeStruct((rows, HEAD_COLUMNS + LANES), bf16),
            compiler_params=room,
            cost_estimate=busy,
        )(here, mix, *slabs, tree_kv, bias, messages[0])
        if p:
            out = swap(out, GROUP * p)
        gathered[first, p] = pltpu.with_memory_space_constraint(out, pltpu.VMEM)
    merged = pl.pallas_call(
        functools.partial(merge_kernel, planes=planes),
        in_specs=[block] * len(pieces),
        out_specs=block,
        out_shape=jax.ShapeDtypeStruct((GROUP, owned, HEAD_COLUMNS), bf16),
        compiler_params=room,
        name="merge",
    )(*[gathered[k] for k in sorted(gathered)])
    if chunks == GROUP:
        bundle = pl.pallas_call(
            bundle_kernel,
            in_specs=[block] * 3,
            out_specs=block,
            out_shape=jax.ShapeDtypeStruct((GROUP, owned + 2 * SLOTS, HEAD_COLUMNS), bf16),
            compiler_params=room,
            name="bundle",
        )(merged, keep, other)
        bundle = lax.all_to_all(
            bundle,
            "ctx",
            split_axis=0,
            concat_axis=0,
            tiled=True,
            axis_index_groups=plane_groups,
        )
        bundle = pltpu.with_memory_space_constraint(bundle, pltpu.VMEM)
        return tuple(
            pl.pallas_call(
                functools.partial(last_kernel, key_of=key_of),
                in_specs=[block] * 3,
                out_specs=[block] * 2,
                out_shape=[jax.ShapeDtypeStruct((owned, model), bf16)] * 2,
                compiler_params=room,
                name="last",
            )(bundle, draft_gain[None, :], own_pick)
        )

    own = pl.pallas_call(
        add_kernel,
        in_specs=[block] * 2,
        out_specs=block,
        out_shape=sums(1),
        compiler_params=room,
        name="add",
    )(keep, other)
    joined = [own]
    offsets = [0]
    masks = [(1 << bit,) for bit in reversed(range(inner)) if 1 << bit >= DIRECT]
    masks.append(tuple(range(1, min(DIRECT, chunks))))
    for mask in masks:
        joined = joined + [swap(x, m) for m in mask for x in joined]
        offsets = offsets + [o ^ m for m in mask for o in offsets]
    joined = [pltpu.with_memory_space_constraint(x, pltpu.VMEM) for x in joined]
    draft_input = pl.pallas_call(
        functools.partial(norm_kernel, offsets=tuple(offsets)),
        in_specs=[scalar] + [block] * (chunks + 2),
        out_specs=block,
        out_shape=jax.ShapeDtypeStruct((owned, model), bf16),
        compiler_params=room,
        name="norm",
    )((me % chunks).astype(jnp.int32)[None], draft_gain[None, :], own_pick, *joined)

    by_seat = lax.all_to_all(
        merged,
        "ctx",
        split_axis=0,
        concat_axis=0,
        tiled=True,
        axis_index_groups=plane_groups,
    )
    seat_of = [key_of.index(k) for k in range(GROUP)]
    attended = jnp.concatenate([by_seat[w] for w in seat_of], axis=1)
    return (attended, draft_input)


def solution(mesh):
    placed = (
        P(("groups", "ctx"), None),
        P(("groups", "ctx"), None),
        P(("groups", "ctx"), None),
        P(("groups", "ctx"), None),
        P(("groups", "ctx"), None),
        P(("groups", "ctx"), None),
        P("ctx", None),
        P("ctx", None),
        P(),
        P("groups", None),
        P("groups"),
    )
    return jax.shard_map(
        body,
        mesh=mesh,
        in_specs=placed,
        out_specs=(P(("groups", "ctx"), None), P(("groups", "ctx"), None)),
        check_vma=False,
    )
```

```python
import functools
import math

import jax
import jax.numpy as jnp
from jax import lax
from jax.experimental import pallas as pl
from jax.experimental.pallas import tpu as pltpu
from jax.sharding import PartitionSpec as P


QUERY_HEADS = 64
KEY_HEADS = 8
HEAD_WIDTH = 128
PER_KEY = QUERY_HEADS // KEY_HEADS
SLOTS = 8
LANES = 128
GROUP = KEY_HEADS
HEAD_COLUMNS = PER_KEY * HEAD_WIDTH
DIRECT = 8
ROOM = 14 * 2**20
STEP = 32
ARRIVAL = (0, 4, 2, 5, 3, 6, 7, 1)
NEGATIVE = -1e30
LOG2_SCALE = HEAD_WIDTH**-0.5 * math.log2(math.e)

f32 = jnp.float32
bf16 = jnp.bfloat16


def dot_t(a, b):
    return lax.dot_general(a, b, (((1,), (1,)), ((), ())), preferred_element_type=f32)


def dot(a, b):
    return lax.dot_general(a, b, (((1,), (0,)), ((), ())), preferred_element_type=f32)


def attend(q, slabs, positions, tree_kv, bias):
    scores = [dot_t(q, s[0:positions, 0:HEAD_WIDTH]) for s in slabs]
    scores.append(dot_t(q, tree_kv[:, 0:HEAD_WIDTH]) + bias)
    top = scores[-1].max(axis=1, keepdims=True)
    for s in scores[:-1]:
        top = jnp.maximum(top, s.max(axis=1, keepdims=True))
    den = jnp.zeros_like(top)
    num = jnp.zeros((q.shape[0], HEAD_WIDTH), f32)
    values = [s[0:positions, HEAD_WIDTH : 2 * HEAD_WIDTH] for s in slabs]
    values.append(tree_kv[:, HEAD_WIDTH : 2 * HEAD_WIDTH])
    for s, v in zip(scores, values):
        w = jnp.exp2((s - top) * LOG2_SCALE)
        den = den + w.sum(axis=1, keepdims=True)
        num = num + dot(w.astype(bf16), v)
    return num / den, top * LOG2_SCALE + jnp.log2(den)


def stack_heads(q):
    q = q.astype(f32)
    return jnp.concatenate(
        [q[:, h * HEAD_WIDTH : (h + 1) * HEAD_WIDTH] for h in range(PER_KEY)], axis=0
    ).astype(bf16)


def bulk_kernel(place_ref, mix_ref, *refs, distance, first, plane_rows, positions):
    slabs = refs[:GROUP]
    tree_ref, bias_ref = refs[GROUP : GROUP + 2]
    out_ref = refs[-1]
    rows = out_ref.shape[0]
    step = min(rows, STEP)
    for tile in range(0, rows, step):
        start = pl.multiple_of((place_ref[0] ^ distance) * plane_rows + first + tile, step)
        q = stack_heads(mix_ref[pl.ds(start, step), 0:HEAD_COLUMNS])
        bias = jnp.concatenate([bias_ref[pl.ds(start, step), :]] * PER_KEY, axis=0)
        out, lse = attend(q, slabs, positions, tree_ref, bias)
        lane = lax.broadcasted_iota(jnp.int32, (step, LANES), 1)
        stats = jnp.zeros((step, LANES), f32)
        piece = slice(tile, tile + step)
        for h in range(PER_KEY):
            part = slice(h * step, (h + 1) * step)
            column = slice(h * HEAD_WIDTH, (h + 1) * HEAD_WIDTH)
            out_ref[piece, column] = out[part].astype(bf16)
            high = lse[part].astype(bf16).astype(f32)
            middle = (lse[part] - high).astype(bf16).astype(f32)
            low = lse[part] - high - middle
            stats = jnp.where(lane == h, high, stats)
            stats = jnp.where(lane == PER_KEY + h, middle, stats)
            stats = jnp.where(lane == 2 * PER_KEY + h, low, stats)
        out_ref[piece, HEAD_COLUMNS : HEAD_COLUMNS + LANES] = stats.astype(bf16)


def accepted_kernel(place_ref, mix_ref, *refs, planes, positions, feat):
    slabs = refs[:GROUP]
    tree_ref, bias_ref, pick_ref = refs[GROUP : GROUP + 3]
    outs = refs[GROUP + 3 : GROUP + 3 + planes]
    hold_ref = refs[GROUP + 3 + planes]
    rows = pick_ref.shape[0]
    q = stack_heads(dot(pick_ref[...], mix_ref[:, 0:HEAD_COLUMNS]))
    bias = jnp.concatenate([bias_ref[...]] * PER_KEY, axis=0)
    out, lse = attend(q, slabs, positions, tree_ref, bias)
    lane = lax.broadcasted_iota(jnp.int32, (rows, LANES), 1)
    stats = [jnp.zeros((rows, LANES), f32) for _ in range(planes)]
    for h in range(PER_KEY):
        chunk, start = h * HEAD_WIDTH // feat, h * HEAD_WIDTH % feat
        part = slice(h * rows, (h + 1) * rows)
        hold_ref[chunk, :, start : start + HEAD_WIDTH] = out[part]
        stats[chunk] = jnp.where(lane == start // HEAD_WIDTH, lse[part], stats[chunk])
    for chunk in range(planes):
        hold_ref[chunk, :, feat : feat + LANES] = stats[chunk]
    for k in range(planes):
        outs[k][...] = hold_ref[place_ref[0] ^ k]


def merge_head(parts, logs):
    top = functools.reduce(jnp.maximum, logs)
    weights = [jnp.exp2(s - top) for s in logs]
    den = functools.reduce(jnp.add, weights)
    num = functools.reduce(jnp.add, [w * p for w, p in zip(weights, parts)])
    return num / den


def merge_kernel(*refs, planes):
    out_ref = refs[-1]
    owned = out_ref.shape[1]
    for first in range(0, len(refs) - 1, planes):
        mine = refs[first : first + planes]
        rows = mine[0].shape[0]
        devices = slice(first // planes * rows // owned, (first // planes + 1) * rows // owned)
        stats = [m[:, HEAD_COLUMNS : HEAD_COLUMNS + LANES].astype(f32) for m in mine]
        for h in range(PER_KEY):
            logs = [
                s[:, h : h + 1]
                + s[:, PER_KEY + h : PER_KEY + h + 1]
                + s[:, 2 * PER_KEY + h : 2 * PER_KEY + h + 1]
                for s in stats
            ]
            column = slice(h * HEAD_WIDTH, (h + 1) * HEAD_WIDTH)
            merged = merge_head([m[:, column].astype(f32) for m in mine], logs)
            out_ref[devices, :, column] = merged.reshape(-1, owned, HEAD_WIDTH).astype(bf16)


def mix_kernel(query_ref, embed_ref, after_ref, out_ref, sems, *, key_of):
    size = out_ref.shape[0]
    feat = embed_ref.shape[1] // size
    copies = []
    for d in range(size):
        start = key_of[d % GROUP] * HEAD_COLUMNS
        pairs = (
            (query_ref.at[:, start : start + HEAD_COLUMNS], pl.ds(0, HEAD_COLUMNS)),
            (embed_ref.at[:, d * feat : (d + 1) * feat], pl.ds(HEAD_COLUMNS, feat)),
        )
        for i, (source, columns) in enumerate(pairs):
            copies.append(
                pltpu.make_async_copy(source, out_ref.at[d, :, columns], sems.at[2 * d + i])
            )
    for c in copies:
        c.start()
    for c in copies:
        c.wait()


def split_kernel(place_ref, keys_ref, values_ref, tree_keys_ref, tree_values_ref, *refs, seats):
    outs, sems = refs[-len(seats) - 1 : -1], refs[-1]
    positions, owned = keys_ref.shape[0], tree_keys_ref.shape[0]
    copies = []
    for i, r in enumerate(seats):
        seat = place_ref[1] ^ r
        head = (seat >> 1) | ((seat & 1) * (GROUP // 2))
        start = pl.multiple_of(head * HEAD_WIDTH, HEAD_WIDTH)
        for j, (x, y) in enumerate(
            ((keys_ref, tree_keys_ref), (values_ref, tree_values_ref))
        ):
            columns = pl.ds(j * HEAD_WIDTH, HEAD_WIDTH)
            for k, (source, first, rows) in enumerate(((x, 0, positions), (y, positions, owned))):
                copies.append(
                    pltpu.make_async_copy(
                        source.at[:, pl.ds(start, HEAD_WIDTH)],
                        outs[i].at[pl.ds(first, rows), columns],
                        sems.at[4 * i + 2 * j + k],
                    )
                )
    for c in copies:
        c.start()
    for c in copies:
        c.wait()


def join(rows, weight, out_ref, base_ref=None, *, trees, spots):
    _, slots, part = out_ref.shape
    chunks = len(spots) // trees
    for n in range(chunks):
        total = dot(rows, weight[:, n * part : (n + 1) * part])
        for t in range(trees):
            spot = spots[t * chunks + n]
            some = total[t * slots : (t + 1) * slots]
            out_ref[spot] = some if base_ref is None else some + base_ref[spot]


def take_halves(bit, keep_ref, send_ref, *refs):
    half = keep_ref.shape[0]
    for ref, start in ((keep_ref, bit * half), (send_ref, (1 - bit) * half)):
        parts = [r[pl.ds(start, half)] for r in refs]
        ref[...] = functools.reduce(jnp.add, parts)


def halve_kernel(bit_ref, mine_ref, other_ref, keep_ref, send_ref):
    take_halves(bit_ref[0], keep_ref, send_ref, mine_ref, other_ref)


def add_kernel(mine_ref, other_ref, out_ref):
    out_ref[...] = mine_ref[...] + other_ref[...]


def embed_kernel(pick_ref, mix_ref, weight_ref, out_ref, *, trees, spots):
    rows = dot(pick_ref[...], mix_ref[:, HEAD_COLUMNS:]).astype(bf16)
    join(rows, weight_ref, out_ref, trees=trees, spots=spots)


def feature_kernel(bit_ref, *refs, planes, feat, trees, spots):
    messages = refs[:planes]
    weight_ref, add_ref, keep_ref, send_ref, hold_ref = refs[planes:]
    heads = []
    for h in range(feat // HEAD_WIDTH):
        column = slice(h * HEAD_WIDTH, (h + 1) * HEAD_WIDTH)
        merged = merge_head(
            [m[:, column] for m in messages],
            [m[:, feat + h : feat + h + 1] for m in messages],
        )
        heads.append(merged.astype(bf16))
    rows = heads[0] if len(heads) == 1 else jnp.concatenate(heads, axis=1)
    join(rows, weight_ref, hold_ref, add_ref, trees=trees, spots=spots)
    take_halves(bit_ref[0], keep_ref, send_ref, hold_ref)


def norm_kernel(place_ref, gain_ref, pick_ref, *refs, offsets):
    joined, out_ref = refs[:-1], refs[-1]
    chunks = len(joined)
    _, slots, width = joined[0].shape
    total = jnp.zeros((slots, width), f32)
    for x in joined:
        total = total + x[0] * x[0]
    total = jnp.sum(total, axis=1, keepdims=True)
    factor = lax.rsqrt(total / (chunks * width) + 1e-06)
    pick = pick_ref[...]
    for x, offset in zip(joined, offsets):
        columns = pl.ds(pl.multiple_of((place_ref[0] ^ offset) * width, width), width)
        normed = x[0] * factor * gain_ref[:, columns]
        rows = jnp.zeros((pick.shape[0], width), f32)
        for s in range(slots):
            rows = rows + jnp.where(pick[:, s : s + 1] > 0.5, normed[s : s + 1, :], 0.0)
        out_ref[:, columns] = rows.astype(bf16)


def bundle_kernel(merged_ref, mine_ref, other_ref, out_ref):
    devices, owned, _ = merged_ref.shape
    total = mine_ref[0] + other_ref[0]
    high = total.astype(bf16)
    low = (total - high.astype(f32)).astype(bf16)
    for d in range(devices):
        out_ref[d, 0:owned] = merged_ref[d]
        out_ref[d, owned : owned + SLOTS] = high
        out_ref[d, owned + SLOTS : owned + 2 * SLOTS] = low


def last_kernel(bundle_ref, gain_ref, pick_ref, attended_ref, draft_ref, *, key_of):
    devices, _, width = bundle_ref.shape
    owned = attended_ref.shape[0]
    joined = []
    total = jnp.zeros((SLOTS, width), f32)
    for d in range(devices):
        columns = slice(key_of[d] * width, (key_of[d] + 1) * width)
        attended_ref[:, columns] = bundle_ref[d, 0:owned]
        high = bundle_ref[d, owned : owned + SLOTS].astype(f32)
        low = bundle_ref[d, owned + SLOTS : owned + 2 * SLOTS].astype(f32)
        joined.append(high + low)
        total = total + joined[d] * joined[d]
    total = jnp.sum(total, axis=1, keepdims=True)
    factor = lax.rsqrt(total / (devices * width) + 1e-06)
    pick = pick_ref[...]
    for d in range(devices):
        columns = slice(d * width, (d + 1) * width)
        normed = joined[d] * factor * gain_ref[:, columns]
        rows = jnp.zeros((pick.shape[0], width), f32)
        for s in range(SLOTS):
            rows = rows + jnp.where(pick[:, s : s + 1] > 0.5, normed[s : s + 1, :], 0.0)
        draft_ref[:, columns] = rows.astype(bf16)


def ancestors(parents):
    nodes = parents.shape[1]
    column = jnp.arange(nodes, dtype=jnp.int32)
    upward = (parents[:, :, None] == column[None, None, :]).astype(f32)
    closure = jnp.maximum(upward, jnp.eye(nodes, dtype=f32)[None])
    for _ in range(3):
        closure = jnp.minimum(jnp.einsum("tij,tjk->tik", closure, closure), 1.0)
    return closure


def body(
    queries,
    prefix_key_heads,
    prefix_value_heads,
    tree_key_heads,
    tree_value_heads,
    token_embed,
    fc_embed,
    fc_feature,
    draft_gain,
    parents,
    accepted,
):
    size = lax.axis_size("ctx")
    me = lax.axis_index("ctx")
    trees, nodes = parents.shape
    owned, model = queries.shape
    positions = prefix_key_heads.shape[0]
    feat = fc_feature.shape[0]
    every_row = trees * nodes
    planes = size // GROUP
    plane, seat = me // GROUP, me % GROUP
    plane_rows = GROUP * owned
    chunks = size // trees
    part = model // chunks
    mixed = HEAD_COLUMNS + feat
    key_of = [(w >> 1) | ((w & 1) * (GROUP // 2)) for w in range(GROUP)]

    scalar = pl.BlockSpec(memory_space=pltpu.SMEM)
    block = pl.BlockSpec(memory_space=pltpu.VMEM)
    outside = pl.BlockSpec(memory_space=pl.ANY)
    stored = pl.BlockSpec(memory_space=pltpu.HBM)
    busy = pl.CostEstimate(flops=4 * 10**9, bytes_accessed=10**6, transcendentals=10**6)
    room = pltpu.CompilerParams(vmem_limit_bytes=ROOM)

    def swap(x, mask):
        return lax.ppermute(x, "ctx", [(s, s ^ mask) for s in range(size)])

    plane_groups = [[p * GROUP + g for g in range(GROUP)] for p in range(planes)]

    def leave(x):
        return pltpu.with_memory_space_constraint(x, pltpu.HBM)

    place = jnp.stack([plane, seat]).astype(jnp.int32)
    here = plane.astype(jnp.int32)[None]
    sources = [
        leave(x)
        for x in (prefix_key_heads, prefix_value_heads, tree_key_heads, tree_value_heads)
    ]

    def split(seats, after):
        return pl.pallas_call(
            functools.partial(split_kernel, seats=seats),
            in_specs=[scalar] + [stored] * 4 + [outside] * len(after),
            out_specs=[block] * len(seats),
            out_shape=[jax.ShapeDtypeStruct((positions + owned, 2 * HEAD_WIDTH), bf16)]
            * len(seats),
            scratch_shapes=[pltpu.SemaphoreType.DMA((4 * len(seats),))],
            compiler_params=room,
            cost_estimate=busy,
            name="split",
        )(place, *sources, *after)

    first = list(split(ARRIVAL[1:4], ()))
    second = list(split(ARRIVAL[4:7], first[:1]))
    packed = pl.pallas_call(
        functools.partial(mix_kernel, key_of=key_of),
        in_specs=[stored, stored, outside],
        out_specs=block,
        out_shape=jax.ShapeDtypeStruct((size, owned, mixed), bf16),
        scratch_shapes=[pltpu.SemaphoreType.DMA((2 * size,))],
        compiler_params=room,
        cost_estimate=busy,
        name="pack",
    )(leave(queries), leave(token_embed), second[0])
    mix = lax.all_to_all(packed, "ctx", split_axis=0, concat_axis=0, tiled=True)
    mix = pltpu.with_memory_space_constraint(mix.reshape(every_row, mixed), pltpu.VMEM)
    third = list(split(ARRIVAL[7:] + ARRIVAL[:1], [packed]))
    slabs = third[-1:] + first + second + third[:-1]
    for i, r in enumerate(ARRIVAL):
        if r:
            slabs[i] = swap(slabs[i], r)
    tree_kv = jnp.concatenate([s[positions:] for s in slabs], axis=0)
    tree_kv = jnp.pad(tree_kv, ((0, LANES - plane_rows), (0, 0)))
    slabs = [pltpu.with_memory_space_constraint(s, pltpu.VMEM) for s in slabs]

    closure = ancestors(parents)
    chosen = (accepted[:, None] == jnp.arange(nodes, dtype=jnp.int32)[None, :]).astype(f32)
    on_path = jnp.einsum("ti,tij->tj", chosen, closure)
    upto = (jnp.arange(nodes)[:, None] <= jnp.arange(nodes)[None, :]).astype(f32)
    rank = jnp.dot(on_path, upto)
    slot = jnp.arange(1, SLOTS + 1, dtype=f32)
    pick = jnp.where(
        (rank[:, None, :] == slot[None, :, None]) & (on_path[:, None, :] > 0.5), 1.0, 0.0
    )
    same = jnp.eye(trees, dtype=f32)
    pick_rows = (same[:, None, :, None] * pick[:, :, None, :]).reshape(trees * SLOTS, every_row)
    reach = (same[:, None, :, None] * closure[:, :, None, :]).reshape(every_row, every_row)
    row = jnp.arange(every_row, dtype=jnp.int32)
    key = jnp.arange(LANES, dtype=jnp.int32)
    key_seat = seat ^ jnp.array(ARRIVAL, jnp.int32)[jnp.minimum(key // owned, GROUP - 1)]
    key_row = plane * plane_rows + key_seat * owned + key % owned
    key_row = jnp.where(key < plane_rows, key_row, -1)
    keys_hot = (row[:, None] == key_row[None, :]).astype(f32)
    bias = jnp.where(jnp.dot(reach, keys_hot) > 0.5, 0.0, NEGATIVE)
    pick_rows = pick_rows.astype(bf16)
    bias_picked = jnp.where(jnp.dot(jnp.dot(pick_rows, reach), keys_hot) > 0.5, 0.0, NEGATIVE)
    own_tree = (jnp.arange(trees) == me // chunks).astype(f32)
    own_rows = (me * owned + jnp.arange(owned))[:, None] == row[None, :]
    own_pick = jnp.einsum(
        "rj,tsj->rs",
        own_rows.astype(f32),
        pick_rows.astype(f32).reshape(trees, SLOTS, every_row) * own_tree[:, None, None],
    )

    bits = size.bit_length() - 1
    inner = chunks.bit_length() - 1
    order = list(range(bits))
    spots = tuple(
        sum(((d >> bit) & 1) << (bits - 1 - i) for i, bit in enumerate(order))
        for d in range(size)
    )

    def sums(devices):
        return jax.ShapeDtypeStruct((devices, SLOTS, part), f32)

    def bit_of(i):
        return ((me >> order[i]) & 1).astype(jnp.int32)[None]

    embed_part = pl.pallas_call(
        functools.partial(embed_kernel, trees=trees, spots=spots),
        in_specs=[block] * 3,
        out_specs=block,
        out_shape=sums(size),
        compiler_params=room,
        cost_estimate=busy,
        name="embed_join",
    )(pick_rows, mix, fc_embed)

    messages = pl.pallas_call(
        functools.partial(accepted_kernel, planes=planes, positions=positions, feat=feat),
        in_specs=[scalar] + [block] * (GROUP + 4),
        out_specs=[block] * planes,
        out_shape=[jax.ShapeDtypeStruct((trees * SLOTS, feat + LANES), f32)] * planes,
        scratch_shapes=[pltpu.VMEM((planes, trees * SLOTS, feat + LANES), f32)],
        compiler_params=room,
        cost_estimate=busy,
        name="accepted",
    )(here, mix, *slabs, tree_kv, bias_picked, pick_rows)
    arrived = []
    for k in range(planes):
        target = [
            (p * GROUP + w, planes * key_of[w] + (p ^ k))
            for p in range(planes)
            for w in range(GROUP)
        ]
        arrived.append(lax.ppermute(messages[k], "ctx", target))
    arrived = [pltpu.with_memory_space_constraint(x, pltpu.VMEM) for x in arrived]
    keep, send = pl.pallas_call(
        functools.partial(feature_kernel, planes=planes, feat=feat, trees=trees, spots=spots),
        in_specs=[scalar] + [block] * (planes + 2),
        out_specs=[block] * 2,
        out_shape=[sums(size // 2)] * 2,
        scratch_shapes=[pltpu.VMEM((size, SLOTS, part), f32)],
        compiler_params=room,
        name="feature_join",
    )(bit_of(0), *arrived, fc_feature, embed_part)
    for i, bit in enumerate(order):
        other = swap(send, 1 << bit)
        other = pltpu.with_memory_space_constraint(other, pltpu.VMEM)
        if i + 1 < bits:
            keep, send = pl.pallas_call(
                halve_kernel,
                in_specs=[scalar] + [block] * 2,
                out_specs=[block] * 2,
                out_shape=[sums(size >> (i + 2))] * 2,
                compiler_params=room,
                name="halve",
            )(bit_of(i + 1), keep, other)
    rows = min(plane_rows, STEP)
    pieces = [(p, f) for p in [*range(1, planes), 0] for f in range(0, plane_rows, rows)]
    gathered = {}
    for p, first in pieces:
        out = pl.pallas_call(
            functools.partial(
                bulk_kernel,
                distance=p,
                first=first,
                plane_rows=plane_rows,
                positions=positions,
            ),
            in_specs=[scalar] + [block] * (GROUP + 3) + [outside],
            out_specs=block,
            out_shape=jax.ShapeDtypeStruct((rows, HEAD_COLUMNS + LANES), bf16),
            compiler_params=room,
            cost_estimate=busy,
        )(here, mix, *slabs, tree_kv, bias, messages[0])
        if p:
            out = swap(out, GROUP * p)
        gathered[first, p] = pltpu.with_memory_space_constraint(out, pltpu.VMEM)
    merged = pl.pallas_call(
        functools.partial(merge_kernel, planes=planes),
        in_specs=[block] * len(pieces),
        out_specs=block,
        out_shape=jax.ShapeDtypeStruct((GROUP, owned, HEAD_COLUMNS), bf16),
        compiler_params=room,
        name="merge",
    )(*[gathered[k] for k in sorted(gathered)])
    if chunks == GROUP:
        bundle = pl.pallas_call(
            bundle_kernel,
            in_specs=[block] * 3,
            out_specs=block,
            out_shape=jax.ShapeDtypeStruct((GROUP, owned + 2 * SLOTS, HEAD_COLUMNS), bf16),
            compiler_params=room,
            name="bundle",
        )(merged, keep, other)
        bundle = lax.all_to_all(
            bundle,
            "ctx",
            split_axis=0,
            concat_axis=0,
            tiled=True,
            axis_index_groups=plane_groups,
        )
        bundle = pltpu.with_memory_space_constraint(bundle, pltpu.VMEM)
        return tuple(
            pl.pallas_call(
                functools.partial(last_kernel, key_of=key_of),
                in_specs=[block] * 3,
                out_specs=[block] * 2,
                out_shape=[jax.ShapeDtypeStruct((owned, model), bf16)] * 2,
                compiler_params=room,
                name="last",
            )(bundle, draft_gain[None, :], own_pick)
        )

    own = pl.pallas_call(
        add_kernel,
        in_specs=[block] * 2,
        out_specs=block,
        out_shape=sums(1),
        compiler_params=room,
        name="add",
    )(keep, other)
    joined = [own]
    offsets = [0]
    masks = [(1 << bit,) for bit in reversed(range(inner)) if 1 << bit >= DIRECT]
    masks.append(tuple(range(1, min(DIRECT, chunks))))
    for mask in masks:
        joined = joined + [swap(x, m) for m in mask for x in joined]
        offsets = offsets + [o ^ m for m in mask for o in offsets]
    joined = [pltpu.with_memory_space_constraint(x, pltpu.VMEM) for x in joined]
    draft_input = pl.pallas_call(
        functools.partial(norm_kernel, offsets=tuple(offsets)),
        in_specs=[scalar] + [block] * (chunks + 2),
        out_specs=block,
        out_shape=jax.ShapeDtypeStruct((owned, model), bf16),
        compiler_params=room,
        name="norm",
    )((me % chunks).astype(jnp.int32)[None], draft_gain[None, :], own_pick, *joined)

    by_seat = lax.all_to_all(
        merged,
        "ctx",
        split_axis=0,
        concat_axis=0,
        tiled=True,
        axis_index_groups=plane_groups,
    )
    seat_of = [key_of.index(k) for k in range(GROUP)]
    attended = jnp.concatenate([by_seat[w] for w in seat_of], axis=1)
    return (attended, draft_input)


def solution(mesh):
    placed = (
        P(("groups", "ctx"), None),
        P(("groups", "ctx"), None),
        P(("groups", "ctx"), None),
        P(("groups", "ctx"), None),
        P(("groups", "ctx"), None),
        P(("groups", "ctx"), None),
        P("ctx", None),
        P("ctx", None),
        P(),
        P("groups", None),
        P("groups"),
    )
    return jax.shard_map(
        body,
        mesh=mesh,
        in_specs=placed,
        out_specs=(P(("groups", "ctx"), None), P(("groups", "ctx"), None)),
        check_vma=False,
    )
```
